32 devices in a mesh: dp: 8 (over y, x, core), tensor: 4 (over z).
Axes of the slice: x: 2, y: 2, z: 4, core: 2. Of those that a mesh axis runs over, the one named last changes fastest.
Arguments:
- block_in: bfloat16 [8192, 4096], P(('dp', 'tensor')), may hold values from -6 to 6
- out_grad: bfloat16 [8192, 4096], P(('dp', 'tensor')), may hold values from -6 to 6
- segment_ids: int32 [8192], P('dp'), may hold values from 0 to 2, as said below
- positions: int32 [8192], P('dp'), may hold values from 0 to 1023, as said below
- group_token_counts: int32 [8], P('dp'), may hold values from 512 to 1024, as said below
- gain_attn: float32 [4096], replicated, may hold values from 0.1 to 1.9
- w_query: bfloat16 [4096, 4096], P('dp', 'tensor'), may hold values from -0.3125 to 0.3125
- w_key: bfloat16 [4096, 4096], P('dp', 'tensor'), may hold values from -0.3125 to 0.3125
- w_value: bfloat16 [4096, 4096], P('dp', 'tensor'), may hold values from -0.09375 to 0.09375
- w_out: bfloat16 [4096, 4096], P('tensor', 'dp'), may hold values from -0.5 to 0.5
- gain_mlp: float32 [4096], replicated, may hold values from 0.1 to 1.9
- w_gate: bfloat16 [4096, 11008], P('dp', 'tensor'), may hold values from -0.09375 to 0.09375
- w_up: bfloat16 [4096, 11008], P('dp', 'tensor'), may hold values from -0.09375 to 0.09375
- w_down: bfloat16 [11008, 4096], P('tensor', 'dp'), may hold values from -0.0546875 to 0.0546875
Outputs:
- block_out: bfloat16 [8192, 4096], P(('dp', 'tensor'))
- input_grad: bfloat16 [8192, 4096], P(('dp', 'tensor'))
- grad_gain_attn: float32 [4096], replicated
- grad_query: float32 [4096, 4096], P('dp', 'tensor')
- grad_key: float32 [4096, 4096], P('dp', 'tensor')
- grad_value: float32 [4096, 4096], P('dp', 'tensor')
- grad_out: float32 [4096, 4096], P('tensor', 'dp')
- grad_gain_mlp: float32 [4096], replicated
- grad_gate: float32 [4096, 11008], P('dp', 'tensor')
- grad_up: float32 [4096, 11008], P('dp', 'tensor')
- grad_down: float32 [11008, 4096], P('tensor', 'dp')
The draws below stay inside these ranges and needn't reach their ends.
Inputs may be any that keep to these rules, and one draw needn't show every extreme that they name: `segment_ids`: within each group of 1024 rows segment ids never fall; ids 0 and 1 are the group's sequences (1 may be absent) and 2 marks the rows from group_token_counts of that group on, when there are any. In a group whose live rows number 1024 or more, sequence 0 holds at least 1024 rows; otherwise it holds all live rows. Each segment's positions run 0, 1, 2, ... in row order. In every draw some group is one sequence of all 1024 rows. `group_token_counts`: some group is full in every draw.
All inputs are finite; a program needn't handle non-finite values.
Results may differ from the reference program's by a relative error of at most 0.014.
Values may be sent and summed in bfloat16 or wider, within the bound.
No kernel may reach another device: no remote copies, remote signals or barrier semaphores. Data moves between devices by JAX's collectives and lax.ppermute only.
A program may use at most 448 MiB of HBM per device.

```python
import jax
import jax.numpy as jnp
from jax import lax

D = 4096
HEADS = 32
FF = 11008
LONGEST = 1024
HEAD_DIM = 128
GROUP = 1024
GROUPS = 8
TOKENS = 8192


def group_layout(key):
    full_group = jax.random.randint(jax.random.fold_in(key, 7), (), 0, GROUPS)

    def one_layout(group_index):
        sub_key = jax.random.fold_in(jax.random.fold_in(key, 11), group_index)
        count_key, split_key = jax.random.split(sub_key)
        drawn = jax.random.randint(count_key, (), GROUP // 2, GROUP + 1)
        is_full = group_index == full_group
        live_count = jnp.where(is_full, GROUP, drawn).astype(jnp.int32)
        low_len = jnp.minimum(LONGEST, live_count)
        high_len = jnp.maximum(low_len, live_count - 1)
        first_drawn = jax.random.randint(split_key, (), low_len, high_len + 1)
        first_len = jnp.where(is_full, GROUP, first_drawn).astype(jnp.int32)
        row_order = jnp.arange(GROUP).astype(jnp.int32)
        past_first = row_order >= first_len
        past_live = row_order >= live_count
        segment = past_first.astype(jnp.int32) + past_live.astype(jnp.int32)
        seg_start = jnp.where(past_live, live_count, jnp.where(past_first, first_len, 0))
        return (segment, (row_order - seg_start).astype(jnp.int32), live_count)
    segment, position, counts = jax.vmap(one_layout)(jnp.arange(GROUPS).astype(jnp.int32))
    return (segment.reshape(-1), position.reshape(-1), counts)


def draw_segment_ids(key, part):
    return group_layout(key)[0]


def draw_positions(key, part):
    return group_layout(key)[1]


def draw_group_token_counts(key, part):
    return group_layout(key)[2]


def draw_block_in(key, part):
    drawn_rows = jax.random.normal(jax.random.fold_in(key, 101), (TOKENS, D), jnp.float32)
    pairing = jax.random.permutation(jax.random.fold_in(key, 102), GROUPS).astype(jnp.int32)
    col_block = (jnp.arange(D) // (D // GROUPS)).astype(jnp.int32)
    row_group = (jnp.arange(TOKENS) // GROUP).astype(jnp.int32)
    boosted = pairing[row_group][:, None] == col_block[None, :]
    drawn_rows = jnp.clip(jnp.where(boosted, drawn_rows * 3.0, drawn_rows), -6.0, 6.0)
    return drawn_rows.astype(jnp.bfloat16)


def linked_weights(key):
    common = jax.random.normal(jax.random.fold_in(key, 201), (D, D), jnp.float32)
    own_noise = jax.random.normal(jax.random.fold_in(key, 202), (D, D), jnp.float32)
    unit_scale = D ** (-0.5)
    clip_limit = 20.0 * unit_scale
    query_weight = jnp.clip(common * unit_scale, -clip_limit, clip_limit)
    key_weight = jnp.clip(own_noise * unit_scale, -clip_limit, clip_limit)
    return (query_weight, key_weight)


def draw_w_query(key, part):
    return linked_weights(key)[0].astype(jnp.bfloat16)


def draw_w_key(key, part):
    return linked_weights(key)[1].astype(jnp.bfloat16)


def spiked(values, rng, source, target, shards_of, factor):
    owner, partner = [(jnp.arange(values.shape[axis_at]) // (values.shape[axis_at] // shards_of)).reshape([-1 if axis == axis_at else 1 for axis in range(values.ndim)]) for axis_at in (source, target)]
    chosen = jax.random.permutation(rng, shards_of)[partner]
    strong = (owner == chosen) | (owner == (partner + shards_of // 2) % shards_of)
    return jnp.where(strong, factor * values, values)


def levels(stream_key, dims, cuts, low, top_value):
    def one(dim, shards_of):
        heights = jax.random.uniform(jax.random.fold_in(jax.random.fold_in(stream_key, 6), dim), (shards_of,), jnp.float32, low / len(cuts), top_value / len(cuts))
        return jnp.repeat(jnp.exp(heights), dims[dim] // shards_of).reshape((-1,) + (1,) * (len(dims) - dim - 1))

    level = one(*cuts[0])
    for cut in cuts[1:]:
        level = level * one(*cut)
    return level


def normal_values(key, shape, width, most, cuts=(), kind=jnp.bfloat16):
    factor_of = levels(key, shape, cuts, -0.22, 0.18) if cuts else 1.0
    values = jax.random.normal(key, shape, jnp.float32) * width * factor_of
    return jnp.minimum(jnp.maximum(values, -most), most).astype(kind)


def gaussian_with(key, extent, deviation, limit, shards, heavy, dtype=jnp.bfloat16):
    values = deviation * jax.random.normal(key, extent, jnp.float32)
    if shards:
        values = values * levels(key, extent, shards, -0.22, 0.18)
    return jnp.clip(spiked(values, jax.random.fold_in(key, 3), *heavy), -limit, limit).astype(dtype)


def setup_inputs(seed: int = 0) -> dict:
    seeds = jax.random.split(jax.random.key(seed), 15)
    return {
        "block_in": draw_block_in(jax.random.fold_in(seeds[14], 71), 0),
        "out_grad": gaussian_with(seeds[1], (TOKENS, D), 1.0, 6.0, ((0, 32),), (0, 1, 32, 2.75)),
        "segment_ids": draw_segment_ids(jax.random.fold_in(seeds[14], 71), 0),
        "positions": draw_positions(jax.random.fold_in(seeds[14], 71), 0),
        "group_token_counts": draw_group_token_counts(jax.random.fold_in(seeds[14], 71), 0),
        "gain_attn": jnp.clip(1.0 + 0.18 * jax.random.normal(seeds[5], (D,), jnp.float32), 0.1, 1.9),
        "w_query": draw_w_query(jax.random.fold_in(seeds[14], 71), 0),
        "w_key": draw_w_key(jax.random.fold_in(seeds[14], 71), 0),
        "w_value": normal_values(seeds[8], (D, D), D ** -0.5, 0.09375, ((0, 8), (1, 4))),
        "w_out": normal_values(seeds[9], (D, D), (D // 32) ** -0.5, 0.5, ((0, 4), (1, 8))),
        "gain_mlp": jnp.clip(1.0 + 0.18 * jax.random.normal(seeds[10], (D,), jnp.float32), 0.1, 1.9),
        "w_gate": normal_values(seeds[11], (D, FF), D ** -0.5, 0.09375, ((0, 8), (1, 4))),
        "w_up": normal_values(seeds[12], (D, FF), D ** -0.5, 0.09375, ((0, 8), (1, 4))),
        "w_down": normal_values(seeds[13], (FF, D), FF ** -0.5, 0.0546875, ((0, 4), (1, 8))),
    }


EPSILON = 1e-05
ROPE_BASE = 10000.0

def matmul(left, right):
    return jnp.dot(left, right, preferred_element_type=jnp.float32)

def rope_tables(position):
    half_dim = HEAD_DIM // 2
    freq_index = jnp.arange(half_dim).astype(jnp.float32)
    frequency = ROPE_BASE ** (-2.0 * freq_index / HEAD_DIM)
    angles = position.astype(jnp.float32)[:, None] * frequency[None, :]
    cos_tab = jnp.cos(angles)
    sine_tab = jnp.sin(angles)
    return (jnp.concatenate([cos_tab, cos_tab], 1)[:, None, :], jnp.concatenate([sine_tab, sine_tab], 1)[:, None, :])

def rotate(field):
    half_dim = field.shape[-1] // 2
    return jnp.concatenate([-field[..., half_dim:], field[..., :half_dim]], -1)

def rotate_back(field):
    half_dim = field.shape[-1] // 2
    return jnp.concatenate([field[..., half_dim:], -field[..., :half_dim]], -1)

def apply_rope(field, cos_tab, sine_tab):
    return field * cos_tab + rotate(field) * sine_tab

def undo_rope(field, cos_tab, sine_tab):
    return field * cos_tab + rotate_back(field * sine_tab)

def norm_back(layer_in, row_inverse_scale, norm_weight, normalized_gradient):
    standardized_gradient = normalized_gradient * norm_weight
    standardized_rows = layer_in * row_inverse_scale
    layer_gradient = row_inverse_scale * (standardized_gradient - standardized_rows * lax.optimization_barrier(jnp.mean(standardized_gradient * standardized_rows, axis=1, keepdims=True)))
    return (layer_gradient, lax.optimization_barrier(jnp.sum(normalized_gradient * standardized_rows, axis=0)))

def one_group(x_rows, dy_rows, segment, position, live_count, gain_attn, w_query, w_key, w_value, w_out, gain_mlp, w_gate, w_up, w_down):
    group_rows = x_rows.shape[0]
    x_float = x_rows.astype(jnp.float32)
    attn_scale = lax.rsqrt(lax.optimization_barrier(jnp.mean(x_float * x_float, axis=1, keepdims=True)) + EPSILON)
    attn_normed = (x_float * attn_scale * gain_attn).astype(jnp.bfloat16)
    cos_tab, sine_tab = rope_tables(position)

    def split_heads(field):
        return field.reshape(group_rows, HEADS, HEAD_DIM)
    queries = apply_rope(split_heads(matmul(attn_normed, w_query)), cos_tab, sine_tab).astype(jnp.bfloat16)
    keys_all = apply_rope(split_heads(matmul(attn_normed, w_key)), cos_tab, sine_tab).astype(jnp.bfloat16)
    values = split_heads(matmul(attn_normed, w_value)).astype(jnp.bfloat16)
    row_order = jnp.arange(group_rows)
    allowed = (segment[:, None] == segment[None, :]) & (row_order[None, :] <= row_order[:, None])
    score_scale = HEAD_DIM ** (-0.5)

    def scores_of(query_per_head, key_h):
        scores = matmul(query_per_head, key_h.T) * score_scale
        return jnp.where(allowed, scores, -1e+30)

    def head_forward(head_args):
        query_per_head, key_h, value_h = head_args
        scores = scores_of(query_per_head, key_h)
        row_max = lax.optimization_barrier(jnp.max(scores, axis=1, keepdims=True))
        log_total = row_max + jnp.log(lax.optimization_barrier(jnp.sum(jnp.exp(scores - row_max), axis=1, keepdims=True)))
        prob_bf = jnp.exp(scores - log_total).astype(jnp.bfloat16)
        return (matmul(prob_bf, value_h).astype(jnp.bfloat16), log_total)
    q_heads = jnp.swapaxes(queries, 0, 1)
    k_heads = jnp.swapaxes(keys_all, 0, 1)
    v_heads = jnp.swapaxes(values, 0, 1)
    attn_heads, log_totals = lax.map(head_forward, (q_heads, k_heads, v_heads))
    attn = jnp.swapaxes(attn_heads, 0, 1).reshape(group_rows, D)
    resid = x_float + matmul(attn, w_out)
    mlp_scale = lax.rsqrt(lax.optimization_barrier(jnp.mean(resid * resid, axis=1, keepdims=True)) + EPSILON)
    mlp_normed = (resid * mlp_scale * gain_mlp).astype(jnp.bfloat16)
    gate_pre = matmul(mlp_normed, w_gate)
    up_pre = matmul(mlp_normed, w_up)
    sigmoid_gate = jax.nn.sigmoid(gate_pre)
    silu_gate = gate_pre * sigmoid_gate
    hidden = (silu_gate * up_pre).astype(jnp.bfloat16)
    block_out = (resid + matmul(hidden, w_down)).astype(jnp.bfloat16)
    live = (row_order < live_count).astype(jnp.bfloat16)
    live_grad = dy_rows * live[:, None]
    d_hidden = matmul(live_grad, w_down.T)
    grad_down = matmul(hidden.T, live_grad)
    d_gate = (d_hidden * up_pre * sigmoid_gate * (1.0 + gate_pre * (1.0 - sigmoid_gate))).astype(jnp.bfloat16)
    d_up = (d_hidden * silu_gate).astype(jnp.bfloat16)
    grad_gate = matmul(mlp_normed.T, d_gate)
    grad_up = matmul(mlp_normed.T, d_up)
    d_norm_mlp = matmul(d_gate, w_gate.T) + matmul(d_up, w_up.T)
    d_from_mlp, grad_gain_mlp = norm_back(resid, mlp_scale, gain_mlp, d_norm_mlp)
    d_resid = live_grad.astype(jnp.float32) + d_from_mlp
    d_resid_b = d_resid.astype(jnp.bfloat16)
    grad_out = matmul(attn.T, d_resid_b)
    d_attn = split_heads(matmul(d_resid_b, w_out.T).astype(jnp.bfloat16))

    def head_backward(head_args):
        query_per_head, key_h, value_h, out_h, dout_h, total_h = head_args
        scores = scores_of(query_per_head, key_h)
        prob_full = jnp.exp(scores - total_h)
        row_delta = lax.optimization_barrier(jnp.sum(dout_h.astype(jnp.float32) * out_h.astype(jnp.float32), axis=1, keepdims=True))
        d_probs = matmul(dout_h, value_h.T)
        d_scores = (prob_full * (d_probs - row_delta) * score_scale).astype(jnp.bfloat16)
        d_value_h = matmul(prob_full.astype(jnp.bfloat16).T, dout_h).astype(jnp.bfloat16)
        return (matmul(d_scores, key_h), matmul(d_scores.T, query_per_head), d_value_h)
    d_q_h, d_k_h, d_v_h = lax.map(head_backward, (q_heads, k_heads, v_heads, attn_heads, jnp.swapaxes(d_attn, 0, 1), log_totals))
    d_queries = undo_rope(jnp.swapaxes(d_q_h, 0, 1), cos_tab, sine_tab).astype(jnp.bfloat16).reshape(group_rows, D)
    d_keys = undo_rope(jnp.swapaxes(d_k_h, 0, 1), cos_tab, sine_tab).astype(jnp.bfloat16).reshape(group_rows, D)
    d_values = jnp.swapaxes(d_v_h, 0, 1).reshape(group_rows, D)
    grad_query = matmul(attn_normed.T, d_queries)
    grad_key = matmul(attn_normed.T, d_keys)
    grad_value = matmul(attn_normed.T, d_values)
    d_norm_attn = matmul(d_queries, w_query.T) + matmul(d_keys, w_key.T) + matmul(d_values, w_value.T)
    d_from_attn, grad_gain_attn = norm_back(x_float, attn_scale, gain_attn, d_norm_attn)
    input_grad = (d_resid + d_from_attn).astype(jnp.bfloat16)
    return ((block_out, input_grad), (grad_gain_attn, grad_query, grad_key, grad_value, grad_out, grad_gain_mlp, grad_gate, grad_up, grad_down))

def reference(block_in, out_grad, segment_ids, positions, group_token_counts, gain_attn, w_query, w_key, w_value, w_out, gain_mlp, w_gate, w_up, w_down):
    x_groups = block_in.reshape(GROUPS, GROUP, D)
    dy_groups = out_grad.reshape(GROUPS, GROUP, D)
    seg_groups = segment_ids.reshape(GROUPS, GROUP)
    pos_groups = positions.reshape(GROUPS, GROUP)
    initial = (jnp.zeros((D,), jnp.float32), jnp.zeros((D, D), jnp.float32), jnp.zeros((D, D), jnp.float32), jnp.zeros((D, D), jnp.float32), jnp.zeros((D, D), jnp.float32), jnp.zeros((D,), jnp.float32), jnp.zeros((D, FF), jnp.float32), jnp.zeros((D, FF), jnp.float32), jnp.zeros((FF, D), jnp.float32))

    def group_step(running, group_item):
        x_rows, dy_rows, segment, position, live_count = group_item
        results, grads = one_group(x_rows, dy_rows, segment, position, live_count, gain_attn, w_query, w_key, w_value, w_out, gain_mlp, w_gate, w_up, w_down)
        return (tuple((total + part for total, part in zip(running, grads))), results)
    totals, results = lax.scan(group_step, initial, (x_groups, dy_groups, seg_groups, pos_groups, group_token_counts))
    block_out = results[0].reshape(TOKENS, D)
    input_grad = results[1].reshape(TOKENS, D)
    return (block_out, input_grad, totals[0], totals[1], totals[2], totals[3], totals[4], totals[5], totals[6], totals[7], totals[8])
```

```python
import jax
import jax.numpy as jnp
from jax import lax
from jax.sharding import PartitionSpec as P

QBLOCKS = 4
HEAD_DIM = 128
EPSILON = 1e-05
ROPE_BASE = 10000.0
BF16 = jnp.bfloat16
F32 = jnp.float32


def matmul(left, right):
    return jnp.dot(left, right, preferred_element_type=F32)


def left_t(left, right):
    return lax.dot_general(left, right, (((0,), (0,)), ((), ())), preferred_element_type=F32)


def right_t(left, right):
    return lax.dot_general(left, right, (((1,), (1,)), ((), ())), preferred_element_type=F32)


def rope_tables(position):
    half_dim = HEAD_DIM // 2
    freq_index = jnp.arange(half_dim).astype(F32)
    frequency = ROPE_BASE ** (-2.0 * freq_index / HEAD_DIM)
    angles = position.astype(F32)[:, None] * frequency[None, :]
    cos_tab = jnp.cos(angles)
    sine_tab = jnp.sin(angles)
    return (
        jnp.concatenate([cos_tab, cos_tab], 1)[:, None, :],
        jnp.concatenate([sine_tab, sine_tab], 1)[:, None, :],
    )


def rotate(field):
    half_dim = field.shape[-1] // 2
    return jnp.concatenate([-field[..., half_dim:], field[..., :half_dim]], -1)


def rotate_back(field):
    half_dim = field.shape[-1] // 2
    return jnp.concatenate([field[..., half_dim:], -field[..., :half_dim]], -1)


def apply_rope(field, cos_tab, sine_tab):
    return field * cos_tab + rotate(field) * sine_tab


def undo_rope(field, cos_tab, sine_tab):
    return field * cos_tab + rotate_back(field * sine_tab)


def norm_back(layer_in, row_inverse_scale, norm_weight, normalized_gradient):
    standardized_gradient = normalized_gradient * norm_weight
    standardized_rows = layer_in * row_inverse_scale
    layer_gradient = row_inverse_scale * (
        standardized_gradient
        - standardized_rows
        * jnp.mean(standardized_gradient * standardized_rows, axis=1, keepdims=True)
    )
    return (layer_gradient, jnp.sum(normalized_gradient * standardized_rows, axis=0))


def line_gather(shard, axis, size):
    if size == 1:
        return shard
    rows = shard.shape[0]
    me = lax.axis_index(axis)
    up = [(k, k + 1) for k in range(size - 1)]
    down = [(k + 1, k) for k in range(size - 1)]
    from_low, from_high = [shard], [shard]
    for step in range(1, size):
        from_low.append(lax.ppermute(from_low[-1], axis, up[step - 1 :]))
        from_high.append(lax.ppermute(from_high[-1], axis, down[: size - step]))
    whole = jnp.zeros((size * rows,) + shard.shape[1:], shard.dtype)
    whole = lax.dynamic_update_slice_in_dim(whole, shard, me * rows, 0)
    for slot in range(1, size):
        piece = jnp.where(me + slot < size, from_high[slot], from_low[size - slot])
        whole = lax.dynamic_update_slice_in_dim(
            whole, piece, lax.rem(me + slot, size) * rows, 0
        )
    return whole


def line_scatter(partial, axis, size):
    rows = partial.shape[0] // size
    me = lax.axis_index(axis)

    def rows_of(owner):
        start = jnp.clip(owner, 0, size - 1) * rows
        return lax.dynamic_slice_in_dim(partial, start, rows, 0).astype(F32)

    if size == 1:
        return partial.astype(F32)
    low = high = None
    for step in range(1, size):
        rise, fall = rows_of(me + size - step), rows_of(me - size + step)
        if step > 1:
            rise = rise + low.astype(F32)
            fall = fall + high.astype(F32)
        up = [(k, k + 1) for k in range(step)]
        down = [(k, k - 1) for k in range(size - step, size)]
        low = lax.ppermute(rise.astype(BF16), axis, up)
        high = lax.ppermute(fall.astype(BF16), axis, down)
    return rows_of(me) + low.astype(F32) + high.astype(F32)


def shards(
    tensor_size,
    block_in,
    out_grad,
    segment_ids,
    positions,
    group_token_counts,
    gain_attn,
    w_query,
    w_key,
    w_value,
    w_out,
    gain_mlp,
    w_gate,
    w_up,
    w_down,
):
    tok_rows = block_in.shape[0]
    query_all, key_all, value_all, out_all = (
        lax.all_gather(w_query, "dp", axis=0, tiled=True),
        lax.all_gather(w_key, "dp", axis=0, tiled=True),
        lax.all_gather(w_value, "dp", axis=0, tiled=True),
        lax.all_gather(w_out, "dp", axis=1, tiled=True),
    )
    gate_all, up_all, down_all = (
        lax.all_gather(w_gate, "dp", axis=0, tiled=True),
        lax.all_gather(w_up, "dp", axis=0, tiled=True),
        lax.all_gather(w_down, "dp", axis=1, tiled=True),
    )

    def gather_rows(rows):
        return line_gather(rows, "tensor", tensor_size)

    def scatter_rows(partial):
        return line_scatter(partial, "tensor", tensor_size)

    x_float = block_in.astype(F32)
    attn_scale = lax.rsqrt(jnp.mean(x_float * x_float, axis=1, keepdims=True) + EPSILON)
    attn_normed = (x_float * attn_scale * gain_attn).astype(BF16)
    whole_attn = gather_rows(attn_normed)
    group_rows = whole_attn.shape[0]
    local_heads = query_all.shape[1] // HEAD_DIM
    cos_tab, sine_tab = rope_tables(positions)

    first_live = lax.axis_index("tensor") * tok_rows
    live = (first_live + jnp.arange(tok_rows) < group_token_counts[0]).astype(BF16)
    live_grad = out_grad * live[:, None]
    whole_grad = gather_rows(lax.optimization_barrier((live_grad, whole_attn))[0])

    def split_heads(field):
        return field.reshape(group_rows, local_heads, HEAD_DIM)

    queries = apply_rope(split_heads(matmul(whole_attn, query_all)), cos_tab, sine_tab).astype(
        BF16
    )
    keys_all = apply_rope(split_heads(matmul(whole_attn, key_all)), cos_tab, sine_tab).astype(BF16)
    values = split_heads(matmul(whole_attn, value_all)).astype(BF16)
    block_rows = group_rows // QBLOCKS
    row_order = jnp.arange(group_rows)
    score_scale = HEAD_DIM ** (-0.5)

    def block_scores(block_index):
        low_row = block_index * block_rows
        high_row = low_row + block_rows
        scores = (
            jnp.einsum(
                "qhd,khd->hqk",
                queries[low_row:high_row],
                keys_all[:high_row],
                preferred_element_type=F32,
            )
            * score_scale
        )
        allowed = (segment_ids[low_row:high_row, None] == segment_ids[None, :high_row]) & (
            row_order[None, :high_row] <= row_order[low_row:high_row, None]
        )
        return jnp.where(allowed[None], scores, -1e30)

    attn_parts = []
    total_parts = []
    for block_index in range(QBLOCKS):
        high_row = (block_index + 1) * block_rows
        scores = block_scores(block_index)
        row_max = jnp.max(scores, axis=2, keepdims=True)
        log_total = row_max + jnp.log(jnp.sum(jnp.exp(scores - row_max), axis=2, keepdims=True))
        prob_bf = jnp.exp(scores - log_total).astype(BF16)
        attn_parts.append(
            jnp.einsum(
                "hqk,khd->qhd", prob_bf, values[:high_row], preferred_element_type=F32
            ).astype(BF16)
        )
        total_parts.append(log_total)
    attn_heads = jnp.concatenate(attn_parts, 0)
    attn = attn_heads.reshape(group_rows, local_heads * HEAD_DIM)
    attn_b, whole_grad = lax.optimization_barrier((attn, whole_grad))
    resid = x_float + scatter_rows(matmul(attn_b, out_all))
    mlp_scale = lax.rsqrt(jnp.mean(resid * resid, axis=1, keepdims=True) + EPSILON)
    mlp_normed = (resid * mlp_scale * gain_mlp).astype(BF16)
    whole_mlp = gather_rows(mlp_normed)
    gate_pre = matmul(whole_mlp, gate_all)
    up_pre = matmul(whole_mlp, up_all)
    sigmoid_gate = jax.nn.sigmoid(gate_pre)
    silu_gate = gate_pre * sigmoid_gate
    hidden = (silu_gate * up_pre).astype(BF16)
    d_hidden = right_t(whole_grad, down_all)
    d_gate = (d_hidden * up_pre * sigmoid_gate * (1.0 + gate_pre * (1.0 - sigmoid_gate))).astype(
        BF16
    )
    d_up = (d_hidden * silu_gate).astype(BF16)
    d_norm_mlp = scatter_rows(right_t(d_gate, gate_all) + right_t(d_up, up_all))
    grad_down_part = left_t(hidden, whole_grad).astype(BF16)
    grad_gate_part = left_t(whole_mlp, d_gate).astype(BF16)
    grad_up_part = left_t(whole_mlp, d_up).astype(BF16)
    d_norm_mlp, grad_down_part, grad_gate_part, grad_up_part = lax.optimization_barrier(
        (d_norm_mlp, grad_down_part, grad_gate_part, grad_up_part)
    )
    d_from_mlp, gain_mlp_part = norm_back(resid, mlp_scale, gain_mlp, d_norm_mlp)
    d_resid = live_grad.astype(F32) + d_from_mlp
    d_resid_b = d_resid.astype(BF16)
    whole_resid = gather_rows(d_resid_b)
    hidden, _ = lax.optimization_barrier((hidden, whole_resid))
    down_rows = scatter_rows(matmul(hidden, down_all))
    grad_out_part = left_t(attn, whole_resid)
    d_attn = split_heads(right_t(whole_resid, out_all).astype(BF16))
    d_q_parts = []
    d_key_sum = jnp.zeros((group_rows, local_heads, HEAD_DIM), F32)
    d_value_sum = jnp.zeros((group_rows, local_heads, HEAD_DIM), F32)
    for block_index in range(QBLOCKS):
        low_row = block_index * block_rows
        high_row = low_row + block_rows
        scores = block_scores(block_index)
        prob_full = jnp.exp(scores - total_parts[block_index])
        dout_rows = d_attn[low_row:high_row]
        row_delta = jnp.sum(
            dout_rows.astype(F32) * attn_heads[low_row:high_row].astype(F32), axis=2
        )
        row_delta = jnp.swapaxes(row_delta, 0, 1)[:, :, None]
        d_probs = jnp.einsum(
            "qhd,khd->hqk", dout_rows, values[:high_row], preferred_element_type=F32
        )
        d_scores = (prob_full * (d_probs - row_delta) * score_scale).astype(BF16)
        d_value_sum = d_value_sum.at[:high_row].add(
            jnp.einsum(
                "hqk,qhd->khd", prob_full.astype(BF16), dout_rows, preferred_element_type=F32
            )
        )
        d_q_parts.append(
            jnp.einsum("hqk,khd->qhd", d_scores, keys_all[:high_row], preferred_element_type=F32)
        )
        d_key_sum = d_key_sum.at[:high_row].add(
            jnp.einsum(
                "hqk,qhd->khd", d_scores, queries[low_row:high_row], preferred_element_type=F32
            )
        )
    local_width = local_heads * HEAD_DIM
    d_queries = (
        undo_rope(jnp.concatenate(d_q_parts, 0), cos_tab, sine_tab)
        .astype(BF16)
        .reshape(group_rows, local_width)
    )
    d_keys = undo_rope(d_key_sum, cos_tab, sine_tab).astype(BF16).reshape(group_rows, local_width)
    d_values = d_value_sum.astype(BF16).reshape(group_rows, local_width)
    d_queries, down_rows = lax.optimization_barrier((d_queries, down_rows))
    block_out = (resid + down_rows).astype(BF16)
    d_norm_attn = scatter_rows(
        right_t(d_queries, query_all) + right_t(d_keys, key_all) + right_t(d_values, value_all)
    )
    grad_query_part = left_t(whole_attn, d_queries)
    grad_key_part = left_t(whole_attn, d_keys)
    grad_value_part = left_t(whole_attn, d_values)
    d_from_attn, gain_attn_part = norm_back(x_float, attn_scale, gain_attn, d_norm_attn)
    input_grad = (d_resid + d_from_attn).astype(BF16)

    def sum_groups(partial, dim):
        return lax.psum_scatter(
            partial.astype(BF16), "dp", scatter_dimension=dim, tiled=True
        ).astype(F32)

    grad_down = sum_groups(grad_down_part, 1)
    grad_gate = sum_groups(grad_gate_part, 0)
    grad_up = sum_groups(grad_up_part, 0)
    grad_out = sum_groups(grad_out_part, 1)
    grad_query = sum_groups(grad_query_part, 0)
    grad_key = sum_groups(grad_key_part, 0)
    grad_value = sum_groups(grad_value_part, 0)
    grad_gain_attn, grad_gain_mlp = lax.psum((gain_attn_part, gain_mlp_part), ("dp", "tensor"))
    return (
        block_out,
        input_grad,
        grad_gain_attn,
        grad_query,
        grad_key,
        grad_value,
        grad_out,
        grad_gain_mlp,
        grad_gate,
        grad_up,
        grad_down,
    )


def solution(mesh):
    tensor_size = mesh.shape["tensor"]
    rows = P(("dp", "tensor"), None)
    into, outof = P("dp", "tensor"), P("tensor", "dp")
    return jax.shard_map(
        lambda *args: shards(tensor_size, *args),
        mesh=mesh,
        in_specs=(
            (rows, rows, P("dp"), P("dp"), P("dp"), P())
            + (into, into, into, outof, P(), into, into, outof)
        ),
        out_specs=(rows, rows, P(), into, into, into, outof, P(), into, into, outof),
        check_vma=False,
    )
```

```python
import jax
import jax.numpy as jnp
import numpy as np
from jax import lax
from jax.experimental import pallas as pl
from jax.experimental.pallas import tpu as pltpu
from jax.sharding import PartitionSpec as P

HEAD_DIM = 128
EPSILON = 1e-05
ROPE_BASE = 10000.0
BF16 = jnp.bfloat16
F32 = jnp.float32
ATTN_ROWS = 256
MASKED = -1e30
STREAMS = 2
TILE = 256


def matmul(left, right):
    return jnp.dot(left, right, preferred_element_type=F32)


def allowed_keys(seg_rows, seg_cols, low, high):
    shape = (high - low, high)
    row = lax.broadcasted_iota(jnp.int32, shape, 0) + low
    col = lax.broadcasted_iota(jnp.int32, shape, 1)
    return (seg_rows[low:high, :] == seg_cols[:, :high]) & (col <= row)


def nt_dot(left, right):
    return lax.dot_general(left, right, (((1,), (1,)), ((), ())), preferred_element_type=F32)


def tn_dot(left, right):
    return lax.dot_general(left, right, (((0,), (0,)), ((), ())), preferred_element_type=F32)


def attn_forward_kernel(qkv_ref, cos_ref, sin_ref, segr_ref, segc_ref, out_ref, kept_ref, lse_ref):
    head = pl.program_id(0)
    rows = qkv_ref.shape[0]
    half = HEAD_DIM // 2
    for part in range(2):
        at = slice(part * HEAD_DIM, (part + 1) * HEAD_DIM)
        raw = qkv_ref[:, at]
        turned = raw * cos_ref[...] + pltpu.roll(raw, half, 1) * sin_ref[...]
        kept_ref[:, at] = turned.astype(BF16)
    kept_ref[:, 2 * HEAD_DIM :] = qkv_ref[:, 2 * HEAD_DIM :].astype(BF16)

    @pl.when(head == 0)
    def _():
        lse_ref[...] = jnp.zeros_like(lse_ref)

    block = min(ATTN_ROWS, rows)
    for low in range(0, rows, block):
        high = low + block
        query = kept_ref[low:high, :HEAD_DIM]
        key = kept_ref[:high, HEAD_DIM : 2 * HEAD_DIM]
        value = kept_ref[:high, 2 * HEAD_DIM :]
        scores = nt_dot(query, key) * HEAD_DIM**-0.5
        scores = jnp.where(allowed_keys(segr_ref, segc_ref, low, high), scores, MASKED)
        top = jnp.max(scores, axis=1, keepdims=True)
        weight = jnp.exp(scores - top)
        total = jnp.sum(weight, axis=1, keepdims=True)
        mixed = jnp.dot(weight.astype(BF16), value, preferred_element_type=F32) / total
        out_ref[low:high, :] = mixed.astype(BF16)
        lane = lax.broadcasted_iota(jnp.int32, (block, HEAD_DIM), 1)
        lse_ref[low:high, :] = jnp.where(lane == head, top + jnp.log(total), lse_ref[low:high, :])


def attn_backward_kernel(
    kept_ref, out_ref, dout_ref, lse_ref, cos_ref, sin_ref, segr_ref, segc_ref, grad_ref, dk_ref, dv_ref
):
    head = pl.program_id(0)
    rows = kept_ref.shape[0]
    half = HEAD_DIM // 2
    scale = HEAD_DIM**-0.5
    block = min(ATTN_ROWS, rows)

    def unturn(grad):
        return grad * cos_ref[...] + pltpu.roll(grad * sin_ref[...], half, 1)

    for low in reversed(range(0, rows, block)):
        high = low + block
        query = kept_ref[low:high, :HEAD_DIM]
        key = kept_ref[:high, HEAD_DIM : 2 * HEAD_DIM]
        value = kept_ref[:high, 2 * HEAD_DIM :]
        dout = dout_ref[low:high, :]
        lane = lax.broadcasted_iota(jnp.int32, (block, HEAD_DIM), 1)
        lse = jnp.sum(jnp.where(lane == head, lse_ref[low:high, :], 0.0), axis=1, keepdims=True)
        delta = jnp.sum(dout.astype(F32) * out_ref[low:high, :].astype(F32), axis=1, keepdims=True)
        scores = nt_dot(query, key) * scale - lse
        scores = jnp.where(allowed_keys(segr_ref, segc_ref, low, high), scores, MASKED)
        prob = jnp.exp(scores)
        d_scores = (prob * (nt_dot(dout, value) - delta) * scale).astype(BF16)
        prob = prob.astype(BF16)
        dq = jnp.dot(d_scores, key, preferred_element_type=F32)
        turn = dq * cos_ref[low:high, :] + pltpu.roll(dq * sin_ref[low:high, :], half, 1)
        grad_ref[low:high, :HEAD_DIM] = turn.astype(BF16)
        dk, dv = tn_dot(d_scores, query), tn_dot(prob, dout)
        if high == rows:
            dk_ref[...] = dk
            dv_ref[...] = dv
        else:
            dk_ref[:high, :] += dk
            dv_ref[:high, :] += dv
    grad_ref[:, HEAD_DIM : 2 * HEAD_DIM] = unturn(dk_ref[...]).astype(BF16)
    grad_ref[:, 2 * HEAD_DIM :] = dv_ref[...].astype(BF16)


def attn_specs(rows):
    one = lambda width: pl.BlockSpec((rows, width), lambda h: (0, h))
    fixed = lambda r, c: pl.BlockSpec((r, c), lambda h: (0, 0))
    tables = [fixed(rows, HEAD_DIM), fixed(rows, HEAD_DIM), fixed(rows, 1), fixed(1, rows)]
    return one, fixed, tables


def attn_forward(qkv, cos, sin, seg):
    rows, width = qkv.shape
    heads = width // (3 * HEAD_DIM)
    one, fixed, tables = attn_specs(rows)
    return pl.pallas_call(
        attn_forward_kernel,
        grid=(heads,),
        in_specs=[one(3 * HEAD_DIM)] + tables,
        out_specs=[one(HEAD_DIM), one(3 * HEAD_DIM), fixed(rows, HEAD_DIM)],
        out_shape=[
            jax.ShapeDtypeStruct((rows, heads * HEAD_DIM), BF16),
            jax.ShapeDtypeStruct((rows, width), BF16),
            jax.ShapeDtypeStruct((rows, HEAD_DIM), F32),
        ],
        **big(),
    )(qkv, cos, sin, seg[:, None], seg[None, :])


def attn_backward(kept, out, dout, lse, cos, sin, seg):
    rows, width = kept.shape
    heads = width // (3 * HEAD_DIM)
    one, fixed, tables = attn_specs(rows)
    return pl.pallas_call(
        attn_backward_kernel,
        grid=(heads,),
        in_specs=[one(3 * HEAD_DIM), one(HEAD_DIM), one(HEAD_DIM), fixed(rows, HEAD_DIM)] + tables,
        out_specs=one(3 * HEAD_DIM),
        out_shape=jax.ShapeDtypeStruct((rows, width), BF16),
        scratch_shapes=[pltpu.VMEM((rows, HEAD_DIM), F32)] * 2,
        **big(),
    )(kept, out, dout, lse, cos, sin, seg[:, None], seg[None, :])


def lanes(width):
    return -(-width // 128) * 128


def weight_grad_kernel(pairs, added, order_ref, *refs):
    lefts, rights, out_ref = refs[:pairs], refs[pairs : 2 * pairs], refs[-1]
    width, room = rights[0].shape[1], out_ref.shape[1]
    total = tn_dot(lefts[0][...], rights[0][...])
    for left, right in zip(lefts[1:], rights[1:]):
        total += tn_dot(left[...], right[...])
    if added:
        total += refs[2 * pairs][:, :width].astype(F32)
    out_ref[:, :width] = total.astype(BF16)
    if room > width:
        out_ref[:, width:] = jnp.zeros((out_ref.shape[0], room - width), BF16)


def weight_grad(lefts, rights, order, depth, added=None):
    width = rights[0].shape[1]
    blocks = order.shape[0]
    rows = sum(left.shape[0] for left in lefts)
    specs = [pl.BlockSpec((left.shape[0], depth), lambda i, o: (0, o[i])) for left in lefts]
    specs += [pl.BlockSpec(right.shape, lambda i, o: (0, 0)) for right in rights]
    extra = []
    if added is not None:
        specs.append(pl.BlockSpec((depth, lanes(width)), lambda i, o: (i, 0)))
        extra = [added]
    return pl.pallas_call(
        lambda *refs: weight_grad_kernel(len(lefts), added is not None, *refs),
        grid_spec=pltpu.PrefetchScalarGridSpec(
            num_scalar_prefetch=1,
            grid=(blocks,),
            in_specs=specs,
            out_specs=pl.BlockSpec((depth, lanes(width)), lambda i, o: (i, 0)),
        ),
        out_shape=jax.ShapeDtypeStruct((blocks * depth, lanes(width)), BF16),
        **big(),
    )(order, *lefts, *rights, *extra)


def pack_kernel(*refs):
    *ins, out_ref = refs
    for part, ref in enumerate(ins):
        out_ref[:, part * HEAD_DIM : (part + 1) * HEAD_DIM] = ref[...]


def pack_heads(weights):
    rows, width = weights[0].shape
    count = len(weights)
    return pl.pallas_call(
        pack_kernel,
        grid=(width // HEAD_DIM,),
        in_specs=[pl.BlockSpec((rows, HEAD_DIM), lambda h: (0, h))] * count,
        out_specs=pl.BlockSpec((rows, count * HEAD_DIM), lambda h: (0, h)),
        out_shape=jax.ShapeDtypeStruct((rows, count * width), BF16),
    )(*weights)


def unpack_kernel(ref, *outs):
    for part, out in enumerate(outs):
        out[...] = ref[:, part * HEAD_DIM : (part + 1) * HEAD_DIM].astype(F32)


def unpack_heads(packed):
    rows, width = packed.shape
    span = 3 * HEAD_DIM
    one = pl.BlockSpec((rows, HEAD_DIM), lambda h: (0, h))
    return pl.pallas_call(
        unpack_kernel,
        grid=(width // span,),
        in_specs=[pl.BlockSpec((rows, span), lambda h: (0, h))],
        out_specs=[one] * 3,
        out_shape=[jax.ShapeDtypeStruct((rows, width // 3), F32)] * 3,
    )(packed)


def big():
    return dict(
        compiler_params=pltpu.CompilerParams(
            dimension_semantics=("arbitrary",), vmem_limit_bytes=56 << 20
        ),
        cost_estimate=pl.CostEstimate(flops=1024, bytes_accessed=1024, transcendentals=0),
    )


def mlp_forward_kernel(rows_ref, gate_ref, up_ref, hidden_ref, gate_out, up_out):
    rows = rows_ref[...]
    gate = jnp.dot(rows, gate_ref[...], preferred_element_type=F32)
    up = jnp.dot(rows, up_ref[...], preferred_element_type=F32)
    hidden_ref[...] = (gate * jax.nn.sigmoid(gate) * up).astype(BF16)
    gate_out[...] = gate
    up_out[...] = up


def mlp_forward(rows, gate, up):
    count, depth = rows.shape
    width = gate.shape[1]
    tile = pl.BlockSpec((count, TILE), lambda i: (0, i))
    weight = pl.BlockSpec((depth, TILE), lambda i: (0, i))
    return pl.pallas_call(
        mlp_forward_kernel,
        grid=(pl.cdiv(width, TILE),),
        in_specs=[pl.BlockSpec((count, depth), lambda i: (0, 0)), weight, weight],
        out_specs=[tile] * 3,
        out_shape=[jax.ShapeDtypeStruct((count, width), kind) for kind in (BF16, F32, F32)],
        **big(),
    )(rows, gate, up)


def mlp_backward_kernel(rows_ref, down_ref, gate_ref, up_ref, d_gate_ref, d_up_ref):
    d_hidden = nt_dot(rows_ref[...], down_ref[...])
    gate, up = gate_ref[...], up_ref[...]
    open_gate = jax.nn.sigmoid(gate)
    d_gate_ref[...] = (d_hidden * up * open_gate * (1.0 + gate * (1.0 - open_gate))).astype(BF16)
    d_up_ref[...] = (d_hidden * (gate * open_gate)).astype(BF16)


def mlp_backward(rows, down, gate, up):
    count, depth = rows.shape
    width = down.shape[0]
    tile = pl.BlockSpec((count, TILE), lambda i: (0, i))
    return pl.pallas_call(
        mlp_backward_kernel,
        grid=(pl.cdiv(width, TILE),),
        in_specs=[
            pl.BlockSpec((count, depth), lambda i: (0, 0)),
            pl.BlockSpec((TILE, depth), lambda i: (i, 0)),
            tile,
            tile,
        ],
        out_specs=[tile] * 2,
        out_shape=[jax.ShapeDtypeStruct((count, width), BF16)] * 2,
        **big(),
    )(rows, down, gate, up)


def pair_kernel(first_ref, second_ref, left_ref, right_ref, out_ref):
    total = nt_dot(first_ref[...], left_ref[...]) + nt_dot(second_ref[...], right_ref[...])
    out_ref[...] = total.astype(out_ref.dtype)


def pair_product(first, second, left, right):
    count, depth = first.shape
    width = left.shape[0]
    whole = pl.BlockSpec((count, depth), lambda i: (0, 0))
    weight = pl.BlockSpec((TILE, depth), lambda i: (i, 0))
    return pl.pallas_call(
        pair_kernel,
        grid=(width // TILE,),
        in_specs=[whole, whole, weight, weight],
        out_specs=pl.BlockSpec((count, TILE), lambda i: (0, i)),
        out_shape=jax.ShapeDtypeStruct((count, width), BF16),
        **big(),
    )(first, second, left, right)


def rope_tables(position):
    half_dim = HEAD_DIM // 2
    freq_index = jnp.arange(half_dim).astype(F32)
    frequency = ROPE_BASE ** (-2.0 * freq_index / HEAD_DIM)
    angles = position.astype(F32)[:, None] * frequency[None, :]
    cos, sin = jnp.cos(angles), jnp.sin(angles)
    return jnp.concatenate([cos, cos], 1), jnp.concatenate([-sin, sin], 1)


def norm_back(layer_in, row_inverse_scale, norm_weight, normalized_gradient):
    standardized_gradient = normalized_gradient * norm_weight
    standardized_rows = layer_in * row_inverse_scale
    layer_gradient = row_inverse_scale * (
        standardized_gradient
        - standardized_rows
        * jnp.mean(standardized_gradient * standardized_rows, axis=1, keepdims=True)
    )
    return (layer_gradient, jnp.sum(normalized_gradient * standardized_rows, axis=0))


def after(value, *earlier):
    return lax.optimization_barrier((value,) + earlier)[0]


class Line:
    def __init__(self, axis, size):
        self.axis, self.size = axis, size
        self.me = lax.axis_index(axis)

    def in_order(self, slots):
        rows = slots[0].shape[0]
        whole = jnp.zeros((self.size * rows,) + slots[0].shape[1:], slots[0].dtype)
        for slot, piece in enumerate(slots):
            whole = lax.dynamic_update_slice_in_dim(
                whole, piece, lax.rem(self.me + slot, self.size) * rows, 0
            )
        return whole

    def slots_of(self, whole):
        rows = whole.shape[0] // self.size
        return [
            lax.dynamic_slice_in_dim(whole, lax.rem(self.me + slot, self.size) * rows, rows, 0)
            for slot in range(self.size)
        ]


class Order:
    def __init__(self):
        self.last = ()

    def after(self, *values):
        held = lax.optimization_barrier(tuple(values) + self.last)[: len(values)]
        return held[0] if len(values) == 1 else held

    def mark(self, *values):
        self.last = tuple(values)
        return values[0] if len(values) == 1 else values

    def pin(self, *values):
        held = lax.optimization_barrier(tuple(values) + self.last)[: len(values)]
        return self.mark(*held)


class Ring:
    def __init__(self, line, order, first):
        self.line, self.order, self.taken, self.came = line, order, 0, ()
        self.first = first

    def take(self):
        if self.came:
            self.came = self.order.pin(*self.came)

    def step(self):
        if self.taken < self.line.size - 1:
            self.take()
            self.taken += 1
            self.send(self.taken)
        return self

    def finish(self):
        while self.taken < self.line.size - 1:
            self.step()
        self.take()
        return self.result()


class Gather(Ring):
    def __init__(self, line, order, shard):
        super().__init__(line, order, shard)
        self.low, self.high = [shard], [shard]

    def send(self, step):
        size, axis = self.line.size, self.line.axis
        if self.came:
            self.low[-1], self.high[-1] = self.came
        up = [(k, k + 1) for k in range(step - 1, size - 1)]
        down = [(k + 1, k) for k in range(size - step)]
        self.came = (lax.ppermute(self.low[-1], axis, up), lax.ppermute(self.high[-1], axis, down))
        self.low.append(self.came[0])
        self.high.append(self.came[1])

    def result(self):
        if self.came:
            self.low[-1], self.high[-1] = self.came
        line = self.line
        slots = [self.first]
        for slot in range(1, line.size):
            near = line.me + slot < line.size
            slots.append(jnp.where(near, self.high[slot], self.low[line.size - slot]))
        return slots


class Scatter(Ring):
    def send(self, step):
        size, axis = self.line.size, self.line.axis
        rise, fall = self.first[size - step].astype(F32), self.first[step].astype(F32)
        if self.came:
            rise = rise + self.came[0].astype(F32)
            fall = fall + self.came[1].astype(F32)
        rise, fall = self.order.pin(rise.astype(BF16), fall.astype(BF16))
        low = lax.ppermute(rise, axis, [(k, k + 1) for k in range(step)])
        high = lax.ppermute(fall, axis, [(k, k - 1) for k in range(size - step, size)])
        self.came = (low, high)

    def result(self):
        total = self.first[0].astype(F32)
        for part in self.came:
            total = total + part.astype(F32)
        return total


def rows_of(whole, count):
    rows = whole.shape[0] // count
    return [whole[k * rows : (k + 1) * rows] for k in range(count)]


class Groups:
    def __init__(self, size, order):
        self.size, self.sequence = size, order
        self.chips = size // 2
        self.core = lax.rem(lax.axis_index("dp"), 2)

    def gradient(self, lefts, rights, core, came):
        lefts = list(lefts)
        lefts[0] = self.sequence.after(lefts[0])
        depth = lefts[0].shape[1] // self.size
        blocks = jnp.arange(self.chips, dtype=jnp.int32) * 2 + core
        return self.sequence.mark(weight_grad(lefts, rights, blocks, depth, came))

    def theirs(self, lefts, rights):
        return self.gradient(lefts, rights, 1 - self.core, None)

    def send(self, theirs):
        theirs = self.sequence.after(theirs)
        return lax.ppermute(theirs, "dp", [(k, k ^ 1) for k in range(self.size)])

    def mine(self, lefts, rights, came):
        return self.gradient(lefts, rights, self.core, came)

    def scatter(self, mine):
        mine = self.sequence.after(mine)
        groups = [[2 * chip + core for chip in range(self.chips)] for core in range(2)]
        return lax.psum_scatter(
            mine, "dp", scatter_dimension=0, tiled=True, axis_index_groups=groups
        )


class Total:
    def __init__(self, value, sizes, order):
        self.value, self.order, self.came = value, order, None
        self.rounds = [
            (axis, size, 1 << bit) for axis, size in sizes for bit in range(size.bit_length() - 1)
        ]
        self.step()

    def step(self):
        if self.came is not None:
            self.value = self.order.mark(self.value + self.order.pin(self.came))
            self.came = None
        if self.rounds:
            axis, size, mask = self.rounds.pop(0)
            self.came = lax.ppermute(self.value, axis, [(k, k ^ mask) for k in range(size)])

    def finish(self):
        while self.came is not None:
            self.step()
        return self.value


def shards(
    sizes,
    block_in,
    out_grad,
    segment_ids,
    positions,
    group_token_counts,
    gain_attn,
    w_query,
    w_key,
    w_value,
    w_out,
    gain_mlp,
    w_gate,
    w_up,
    w_down,
):
    order = Order()
    line = Line("tensor", sizes["tensor"])
    groups = Groups(sizes["dp"], order)
    tok_rows, width = block_in.shape
    streams = range(STREAMS)

    qkv_all = lax.all_gather(pack_heads([w_query, w_key, w_value]), "dp", axis=0, tiled=True)
    out_all = lax.all_gather(w_out, "dp", axis=1, tiled=True)
    gate_all = lax.all_gather(w_gate, "dp", axis=0, tiled=True)
    up_all = lax.all_gather(w_up, "dp", axis=0, tiled=True)

    def timed(fn, first, *rest):
        return order.mark(fn(order.after(first), *rest))

    with jax.named_scope("normed_rows"):
        x_float = block_in.astype(F32)
        attn_scale = lax.rsqrt(jnp.mean(x_float * x_float, axis=1, keepdims=True) + EPSILON)
        attn_normed = order.mark((x_float * attn_scale * gain_attn).astype(BF16))
        ring = Gather(line, order, attn_normed).step()
        whole_attn = order.mark(line.in_order(ring.finish()))
    cos, sin = rope_tables(positions)

    with jax.named_scope("live_rows"):
        first_live = lax.axis_index("tensor") * tok_rows
        live = (first_live + jnp.arange(tok_rows) < group_token_counts[0]).astype(BF16)
        live_grad = out_grad * live[:, None]
        live_ring = Gather(line, order, order.after(live_grad)).step()

    with jax.named_scope("attention"):
        qkv = timed(matmul, whole_attn, qkv_all)
        live_ring.step()
        attn, kept, lse = attn_forward(order.after(qkv), cos, sin, segment_ids)
        order.mark(attn)

    attn_slots = line.slots_of(attn)
    attn_of = [
        jnp.concatenate([rows_of(slot, STREAMS)[k] for slot in attn_slots], 0) for k in streams
    ]
    x_of = rows_of(x_float, STREAMS)

    def result(grad, width):
        return order.mark(order.after(grad).astype(F32)[:, :width])

    def row_scale(rows):
        return lax.rsqrt(jnp.mean(rows * rows, axis=1, keepdims=True) + EPSILON)

    resid, mlp_scale, whole_mlp = [], [], []

    def mlp_rows(k, total):
        resid.append(x_of[k] + total)
        mlp_scale.append(row_scale(resid[k]))
        return order.mark((resid[k] * mlp_scale[k] * gain_mlp).astype(BF16))

    with jax.named_scope("resid"):
        parts = [timed(matmul, attn_of[k], out_all) for k in streams]
        live_ring.step()
        ring = Scatter(line, order, rows_of(parts[0], line.size)).step()
        ring.step()
        live_slots = live_ring.finish()
        live_of = [
            jnp.concatenate([rows_of(slot, STREAMS)[k] for slot in live_slots], 0) for k in streams
        ]
        ring.step()
        gate_all = order.pin(gate_all)
        down_all = lax.all_gather(order.after(w_down), "dp", axis=1, tiled=True)
        total = ring.finish()

    with jax.named_scope("mlp_rows"):
        ring = Gather(line, order, mlp_rows(0, total)).step()
        ring.step()
        later = Scatter(line, order, rows_of(parts[1], line.size)).step()
        ring.step()
        later.step()
        whole_mlp.append(jnp.concatenate(ring.finish(), 0))
        later.step()

    hidden, acts, d_gate, d_up, d_sums = [], [], [], [], []

    def forward(k):
        made = order.mark(*mlp_forward(order.after(whole_mlp[k]), gate_all, up_all))
        hidden.append(made[0])
        acts.append(made[1:])

    def backward(k):
        made = order.mark(*mlp_backward(order.after(live_of[k]), down_all, *acts[k]))
        d_gate.append(made[0])
        d_up.append(made[1])

    def scatter_input(k):
        part = timed(pair_product, d_gate[k], d_up[k], gate_all, up_all)
        return Scatter(line, order, rows_of(part, line.size)).step()

    d_resid, gains_mlp, whole_resid = [], [], []
    live_parts = rows_of(live_grad, STREAMS)

    def gather_residual(k):
        back, gain_part = norm_back(resid[k], mlp_scale[k], gain_mlp, d_sums[k])
        gains_mlp.append(gain_part)
        d_resid.append(live_parts[k].astype(F32) + back)
        return Gather(line, order, order.mark(d_resid[k].astype(BF16))).step()

    with jax.named_scope("mlp"):
        forward(0)
        ring = Gather(line, order, mlp_rows(1, later.finish())).step()
        ring.step()
        ring.step()
        whole_mlp.append(jnp.concatenate(ring.finish(), 0))
        forward(1)
        backward(0)
        early = scatter_input(0)
        theirs = groups.theirs(live_of, hidden)
        early.step()
        down_came = groups.send(theirs)
        backward(1)
        early.step()
        part = timed(pair_product, d_gate[1], d_up[1], gate_all, up_all)

    with jax.named_scope("grads_mlp"):
        d_sums.append(early.finish())
        ring = gather_residual(0)
        down_mine = groups.mine(live_of, hidden, down_came)
        theirs = groups.theirs(whole_mlp, d_gate)
        ring.step()
        later = Scatter(line, order, rows_of(part, line.size)).step()
        grad_down = groups.scatter(down_mine)
        gate_came = groups.send(theirs)
        hidden_slots = [rows_of(hidden[k], line.size) for k in streams]
        hidden_rows = jnp.concatenate([part for slot in zip(*hidden_slots) for part in slot], 0)
        down_part = timed(matmul, hidden_rows, down_all)
        ring.step()
        later.step()
        gate_mine = groups.mine(whole_mlp, d_gate, gate_came)
        whole_resid.append(jnp.concatenate(ring.finish(), 0))
        later.step()
        theirs = groups.theirs(whole_mlp, d_up)
        d_sums.append(later.finish())
        ring = gather_residual(1)
        up_came = groups.send(theirs)
        d_attn_of = [timed(nt_dot, whole_resid[0], out_all).astype(BF16)]
        grad_down = order.pin(grad_down)
        grad_gate = groups.scatter(gate_mine)
        ring.step()
        down_ring = Scatter(line, order, rows_of(down_part, line.size)).step()
        up_mine = groups.mine(whole_mlp, d_up, up_came)
        ring.step()
        whole_resid.append(jnp.concatenate(ring.finish(), 0))
        down_ring.step()

    with jax.named_scope("d_attn"):
        d_attn_of.append(timed(nt_dot, whole_resid[1], out_all).astype(BF16))
        d_attn = line.in_order(
            [
                jnp.concatenate(slot, 0)
                for slot in zip(*[rows_of(d_attn_of[k], line.size) for k in streams])
            ]
        )
        order.mark(d_attn)
        grad_gate = order.pin(grad_gate)
        grad_up = groups.scatter(up_mine)
        d_attn = order.after(d_attn)
        d_qkv = order.mark(attn_backward(kept, attn, d_attn, lse, cos, sin, segment_ids))
        down_ring.step()

    with jax.named_scope("grads_attn"):
        qkv_theirs = groups.theirs([whole_attn], [d_qkv])
        qkv_came = groups.send(qkv_theirs)
        out_theirs = groups.theirs(whole_resid, attn_of)
        qkv_mine = groups.mine([whole_attn], [d_qkv], qkv_came)

    with jax.named_scope("d_norm_attn"):
        grad_up = order.pin(grad_up)
        grad_qkv = groups.scatter(qkv_mine)
        d_norm_part = timed(nt_dot, d_qkv, qkv_all)
        down_sum = down_ring.finish()
        ring = Scatter(line, order, line.slots_of(d_norm_part)).step()

    with jax.named_scope("grads_attn"):
        gain_attn_part = order.mark(
            jnp.sum(order.after(d_norm_part) * whole_attn.astype(F32), axis=0) / gain_attn
        )
        everywhere = (("dp", sizes["dp"]), ("tensor", sizes["tensor"]))
        gains = Total(jnp.stack([gain_attn_part, sum(gains_mlp)]), everywhere, order)
        out_came = groups.send(out_theirs)
        grad_down = result(grad_down, w_down.shape[0]).T
        ring.step()
        gains.step()
        out_mine = groups.mine(whole_resid, attn_of, out_came)
        grad_qkv = order.pin(grad_qkv)
        grad_out = groups.scatter(out_mine)
        gains.step()
        grad_gate = result(grad_gate, w_gate.shape[1])
        ring.step()
        gains.step()
        grad_up = result(grad_up, w_up.shape[1])
        gains.step()
        d_norm_attn = ring.finish()

    with jax.named_scope("input_grad"):
        d_from_attn, _ = norm_back(x_float, attn_scale, gain_attn, d_norm_attn)
        input_grad = order.mark((jnp.concatenate(d_resid, 0) + d_from_attn).astype(BF16))
    with jax.named_scope("gains"):
        grad_gains = gains.finish()
        grad_gain_attn, grad_gain_mlp = grad_gains[0], grad_gains[1]

    with jax.named_scope("results"):
        block_out = (jnp.concatenate(resid, 0) + down_sum).astype(BF16)
        grad_query, grad_key, grad_value = unpack_heads(grad_qkv)
        grad_out = grad_out.astype(F32)
    return (
        block_out,
        input_grad,
        grad_gain_attn,
        grad_query,
        grad_key,
        grad_value,
        grad_out.T,
        grad_gain_mlp,
        grad_gate,
        grad_up,
        grad_down,
    )


def solution(mesh):
    sizes = {axis: mesh.shape[axis] for axis in ("dp", "tensor")}
    rows = P(("dp", "tensor"), None)
    into, outof = P("dp", "tensor"), P("tensor", "dp")
    return jax.shard_map(
        lambda *args: shards(sizes, *args),
        mesh=mesh,
        in_specs=(
            (rows, rows, P("dp"), P("dp"), P("dp"), P())
            + (into, into, into, outof, P(), into, into, outof)
        ),
        out_specs=(rows, rows, P(), into, into, into, outof, P(), into, into, outof),
        check_vma=False,
    )
```

```python
import jax
import jax.numpy as jnp
import numpy as np
from jax import lax
from jax.experimental import pallas as pl
from jax.experimental.pallas import tpu as pltpu
from jax.sharding import PartitionSpec as P

HEAD_DIM = 128
EPSILON = 1e-05
ROPE_BASE = 10000.0
BF16 = jnp.bfloat16
F32 = jnp.float32
ATTN_ROWS = 256
MASKED = -1e30
STREAMS = 2
TILE = 256


def matmul(left, right):
    return jnp.dot(left, right, preferred_element_type=F32)


def allowed_keys(seg_rows, seg_cols, low, high):
    shape = (high - low, high)
    row = lax.broadcasted_iota(jnp.int32, shape, 0) + low
    col = lax.broadcasted_iota(jnp.int32, shape, 1)
    return (seg_rows[low:high, :] == seg_cols[:, :high]) & (col <= row)


def nt_dot(left, right):
    return lax.dot_general(left, right, (((1,), (1,)), ((), ())), preferred_element_type=F32)


def tn_dot(left, right):
    return lax.dot_general(left, right, (((0,), (0,)), ((), ())), preferred_element_type=F32)


def attn_forward_kernel(qkv_ref, cos_ref, sin_ref, segr_ref, segc_ref, out_ref, kept_ref, lse_ref):
    head = pl.program_id(0)
    rows = qkv_ref.shape[0]
    half = HEAD_DIM // 2
    for part in range(2):
        at = slice(part * HEAD_DIM, (part + 1) * HEAD_DIM)
        raw = qkv_ref[:, at]
        turned = raw * cos_ref[...] + pltpu.roll(raw, half, 1) * sin_ref[...]
        kept_ref[:, at] = turned.astype(BF16)
    kept_ref[:, 2 * HEAD_DIM :] = qkv_ref[:, 2 * HEAD_DIM :].astype(BF16)

    @pl.when(head == 0)
    def _():
        lse_ref[...] = jnp.zeros_like(lse_ref)

    block = min(ATTN_ROWS, rows)
    for low in range(0, rows, block):
        high = low + block
        query = kept_ref[low:high, :HEAD_DIM]
        key = kept_ref[:high, HEAD_DIM : 2 * HEAD_DIM]
        value = kept_ref[:high, 2 * HEAD_DIM :]
        scores = nt_dot(query, key) * HEAD_DIM**-0.5
        scores = jnp.where(allowed_keys(segr_ref, segc_ref, low, high), scores, MASKED)
        top = jnp.max(scores, axis=1, keepdims=True)
        weight = jnp.exp(scores - top)
        total = jnp.sum(weight, axis=1, keepdims=True)
        mixed = jnp.dot(weight.astype(BF16), value, preferred_element_type=F32) / total
        out_ref[low:high, :] = mixed.astype(BF16)
        lane = lax.broadcasted_iota(jnp.int32, (block, HEAD_DIM), 1)
        lse_ref[low:high, :] = jnp.where(lane == head, top + jnp.log(total), lse_ref[low:high, :])


def attn_backward_kernel(
    kept_ref, out_ref, dout_ref, lse_ref, cos_ref, sin_ref, segr_ref, segc_ref, grad_ref, dk_ref, dv_ref
):
    head = pl.program_id(0)
    rows = kept_ref.shape[0]
    half = HEAD_DIM // 2
    scale = HEAD_DIM**-0.5
    block = min(ATTN_ROWS, rows)

    def unturn(grad):
        return grad * cos_ref[...] + pltpu.roll(grad * sin_ref[...], half, 1)

    for low in reversed(range(0, rows, block)):
        high = low + block
        query = kept_ref[low:high, :HEAD_DIM]
        key = kept_ref[:high, HEAD_DIM : 2 * HEAD_DIM]
        value = kept_ref[:high, 2 * HEAD_DIM :]
        dout = dout_ref[low:high, :]
        lane = lax.broadcasted_iota(jnp.int32, (block, HEAD_DIM), 1)
        lse = jnp.sum(jnp.where(lane == head, lse_ref[low:high, :], 0.0), axis=1, keepdims=True)
        delta = jnp.sum(dout.astype(F32) * out_ref[low:high, :].astype(F32), axis=1, keepdims=True)
        scores = nt_dot(query, key) * scale - lse
        scores = jnp.where(allowed_keys(segr_ref, segc_ref, low, high), scores, MASKED)
        prob = jnp.exp(scores)
        d_scores = (prob * (nt_dot(dout, value) - delta) * scale).astype(BF16)
        prob = prob.astype(BF16)
        dq = jnp.dot(d_scores, key, preferred_element_type=F32)
        turn = dq * cos_ref[low:high, :] + pltpu.roll(dq * sin_ref[low:high, :], half, 1)
        grad_ref[low:high, :HEAD_DIM] = turn.astype(BF16)
        dk, dv = tn_dot(d_scores, query), tn_dot(prob, dout)
        if high == rows:
            dk_ref[...] = dk
            dv_ref[...] = dv
        else:
            dk_ref[:high, :] += dk
            dv_ref[:high, :] += dv
    grad_ref[:, HEAD_DIM : 2 * HEAD_DIM] = unturn(dk_ref[...]).astype(BF16)
    grad_ref[:, 2 * HEAD_DIM :] = dv_ref[...].astype(BF16)


def attn_specs(rows):
    one = lambda width: pl.BlockSpec((rows, width), lambda h: (0, h))
    fixed = lambda r, c: pl.BlockSpec((r, c), lambda h: (0, 0))
    tables = [fixed(rows, HEAD_DIM), fixed(rows, HEAD_DIM), fixed(rows, 1), fixed(1, rows)]
    return one, fixed, tables


def attn_forward(qkv, cos, sin, seg):
    rows, width = qkv.shape
    heads = width // (3 * HEAD_DIM)
    one, fixed, tables = attn_specs(rows)
    return pl.pallas_call(
        attn_forward_kernel,
        grid=(heads,),
        in_specs=[one(3 * HEAD_DIM)] + tables,
        out_specs=[one(HEAD_DIM), one(3 * HEAD_DIM), fixed(rows, HEAD_DIM)],
        out_shape=[
            jax.ShapeDtypeStruct((rows, heads * HEAD_DIM), BF16),
            jax.ShapeDtypeStruct((rows, width), BF16),
            jax.ShapeDtypeStruct((rows, HEAD_DIM), F32),
        ],
        **big(),
    )(qkv, cos, sin, seg[:, None], seg[None, :])


def attn_backward(kept, out, dout, lse, cos, sin, seg):
    rows, width = kept.shape
    heads = width // (3 * HEAD_DIM)
    one, fixed, tables = attn_specs(rows)
    return pl.pallas_call(
        attn_backward_kernel,
        grid=(heads,),
        in_specs=[one(3 * HEAD_DIM), one(HEAD_DIM), one(HEAD_DIM), fixed(rows, HEAD_DIM)] + tables,
        out_specs=one(3 * HEAD_DIM),
        out_shape=jax.ShapeDtypeStruct((rows, width), BF16),
        scratch_shapes=[pltpu.VMEM((rows, HEAD_DIM), F32)] * 2,
        **big(),
    )(kept, out, dout, lse, cos, sin, seg[:, None], seg[None, :])


def lanes(width):
    return -(-width // 128) * 128


def weight_grad_kernel(pairs, added, order_ref, *refs):
    lefts, rights, out_ref = refs[:pairs], refs[pairs : 2 * pairs], refs[-1]
    width, room = rights[0].shape[1], out_ref.shape[1]
    total = tn_dot(lefts[0][...], rights[0][...])
    for left, right in zip(lefts[1:], rights[1:]):
        total += tn_dot(left[...], right[...])
    if added:
        total += refs[2 * pairs][:, :width].astype(F32)
    out_ref[:, :width] = total.astype(BF16)
    if room > width:
        out_ref[:, width:] = jnp.zeros((out_ref.shape[0], room - width), BF16)


def weight_grad(lefts, rights, order, depth, added=None):
    width = rights[0].shape[1]
    blocks = order.shape[0]
    rows = sum(left.shape[0] for left in lefts)
    specs = [pl.BlockSpec((left.shape[0], depth), lambda i, o: (0, o[i])) for left in lefts]
    specs += [pl.BlockSpec(right.shape, lambda i, o: (0, 0)) for right in rights]
    extra = []
    if added is not None:
        specs.append(pl.BlockSpec((depth, lanes(width)), lambda i, o: (i, 0)))
        extra = [added]
    return pl.pallas_call(
        lambda *refs: weight_grad_kernel(len(lefts), added is not None, *refs),
        grid_spec=pltpu.PrefetchScalarGridSpec(
            num_scalar_prefetch=1,
            grid=(blocks,),
            in_specs=specs,
            out_specs=pl.BlockSpec((depth, lanes(width)), lambda i, o: (i, 0)),
        ),
        out_shape=jax.ShapeDtypeStruct((blocks * depth, lanes(width)), BF16),
        **big(),
    )(order, *lefts, *rights, *extra)


def pack_kernel(*refs):
    *ins, out_ref = refs
    for part, ref in enumerate(ins):
        out_ref[:, part * HEAD_DIM : (part + 1) * HEAD_DIM] = ref[...]


def pack_heads(weights):
    rows, width = weights[0].shape
    count = len(weights)
    return pl.pallas_call(
        pack_kernel,
        grid=(width // HEAD_DIM,),
        in_specs=[pl.BlockSpec((rows, HEAD_DIM), lambda h: (0, h))] * count,
        out_specs=pl.BlockSpec((rows, count * HEAD_DIM), lambda h: (0, h)),
        out_shape=jax.ShapeDtypeStruct((rows, count * width), BF16),
    )(*weights)


def unpack_kernel(ref, *outs):
    for part, out in enumerate(outs):
        out[...] = ref[:, part * HEAD_DIM : (part + 1) * HEAD_DIM].astype(F32)


def unpack_heads(packed):
    rows, width = packed.shape
    span = 3 * HEAD_DIM
    one = pl.BlockSpec((rows, HEAD_DIM), lambda h: (0, h))
    return pl.pallas_call(
        unpack_kernel,
        grid=(width // span,),
        in_specs=[pl.BlockSpec((rows, span), lambda h: (0, h))],
        out_specs=[one] * 3,
        out_shape=[jax.ShapeDtypeStruct((rows, width // 3), F32)] * 3,
    )(packed)


def turned_kernel(in_ref, out_ref):
    out_ref[...] = in_ref[...].astype(F32).T


def turned_result(grad, width):
    rows = grad.shape[0]
    return pl.pallas_call(
        turned_kernel,
        grid=(pl.cdiv(width, TILE),),
        in_specs=[pl.BlockSpec((rows, TILE), lambda i: (0, i))],
        out_specs=pl.BlockSpec((TILE, rows), lambda i: (i, 0)),
        out_shape=jax.ShapeDtypeStruct((width, rows), F32),
    )(grad)


def big():
    return dict(
        compiler_params=pltpu.CompilerParams(
            dimension_semantics=("arbitrary",), vmem_limit_bytes=56 << 20
        ),
        cost_estimate=pl.CostEstimate(flops=1024, bytes_accessed=1024, transcendentals=0),
    )


def mlp_forward_kernel(rows_ref, gate_ref, up_ref, hidden_ref, gate_out, up_out):
    rows = rows_ref[...]
    gate = jnp.dot(rows, gate_ref[...], preferred_element_type=F32)
    up = jnp.dot(rows, up_ref[...], preferred_element_type=F32)
    hidden_ref[...] = (gate * jax.nn.sigmoid(gate) * up).astype(BF16)
    gate_out[...] = gate
    up_out[...] = up


def mlp_forward(rows, gate, up):
    count, depth = rows.shape
    width = gate.shape[1]
    tile = pl.BlockSpec((count, TILE), lambda i: (0, i))
    weight = pl.BlockSpec((depth, TILE), lambda i: (0, i))
    return pl.pallas_call(
        mlp_forward_kernel,
        grid=(pl.cdiv(width, TILE),),
        in_specs=[pl.BlockSpec((count, depth), lambda i: (0, 0)), weight, weight],
        out_specs=[tile] * 3,
        out_shape=[jax.ShapeDtypeStruct((count, width), kind) for kind in (BF16, F32, F32)],
        **big(),
    )(rows, gate, up)


def mlp_backward_kernel(rows_ref, down_ref, gate_ref, up_ref, d_gate_ref, d_up_ref):
    d_hidden = nt_dot(rows_ref[...], down_ref[...])
    gate, up = gate_ref[...], up_ref[...]
    open_gate = jax.nn.sigmoid(gate)
    d_gate_ref[...] = (d_hidden * up * open_gate * (1.0 + gate * (1.0 - open_gate))).astype(BF16)
    d_up_ref[...] = (d_hidden * (gate * open_gate)).astype(BF16)


def mlp_backward(rows, down, gate, up):
    count, depth = rows.shape
    width = down.shape[0]
    tile = pl.BlockSpec((count, TILE), lambda i: (0, i))
    return pl.pallas_call(
        mlp_backward_kernel,
        grid=(pl.cdiv(width, TILE),),
        in_specs=[
            pl.BlockSpec((count, depth), lambda i: (0, 0)),
            pl.BlockSpec((TILE, depth), lambda i: (i, 0)),
            tile,
            tile,
        ],
        out_specs=[tile] * 2,
        out_shape=[jax.ShapeDtypeStruct((count, width), BF16)] * 2,
        **big(),
    )(rows, down, gate, up)


def pair_kernel(first_ref, second_ref, left_ref, right_ref, out_ref):
    total = nt_dot(first_ref[...], left_ref[...]) + nt_dot(second_ref[...], right_ref[...])
    out_ref[...] = total.astype(out_ref.dtype)


def pair_product(first, second, left, right):
    count, depth = first.shape
    width = left.shape[0]
    whole = pl.BlockSpec((count, depth), lambda i: (0, 0))
    weight = pl.BlockSpec((TILE, depth), lambda i: (i, 0))
    return pl.pallas_call(
        pair_kernel,
        grid=(width // TILE,),
        in_specs=[whole, whole, weight, weight],
        out_specs=pl.BlockSpec((count, TILE), lambda i: (0, i)),
        out_shape=jax.ShapeDtypeStruct((count, width), BF16),
        **big(),
    )(first, second, left, right)


def rope_tables(position):
    half_dim = HEAD_DIM // 2
    freq_index = jnp.arange(half_dim).astype(F32)
    frequency = ROPE_BASE ** (-2.0 * freq_index / HEAD_DIM)
    angles = position.astype(F32)[:, None] * frequency[None, :]
    cos, sin = jnp.cos(angles), jnp.sin(angles)
    return jnp.concatenate([cos, cos], 1), jnp.concatenate([-sin, sin], 1)


def norm_back(layer_in, row_inverse_scale, norm_weight, normalized_gradient):
    standardized_gradient = normalized_gradient * norm_weight
    standardized_rows = layer_in * row_inverse_scale
    layer_gradient = row_inverse_scale * (
        standardized_gradient
        - standardized_rows
        * jnp.mean(standardized_gradient * standardized_rows, axis=1, keepdims=True)
    )
    return (layer_gradient, jnp.sum(normalized_gradient * standardized_rows, axis=0))


def after(value, *earlier):
    return lax.optimization_barrier((value,) + earlier)[0]


class Line:
    def __init__(self, axis, size):
        self.axis, self.size = axis, size
        self.me = lax.axis_index(axis)

    def in_order(self, slots):
        rows = slots[0].shape[0]
        whole = jnp.zeros((self.size * rows,) + slots[0].shape[1:], slots[0].dtype)
        for slot, piece in enumerate(slots):
            whole = lax.dynamic_update_slice_in_dim(
                whole, piece, lax.rem(self.me + slot, self.size) * rows, 0
            )
        return whole

    def slots_of(self, whole):
        rows = whole.shape[0] // self.size
        return [
            lax.dynamic_slice_in_dim(whole, lax.rem(self.me + slot, self.size) * rows, rows, 0)
            for slot in range(self.size)
        ]


class Order:
    def __init__(self):
        self.last = ()

    def after(self, *values):
        held = lax.optimization_barrier(tuple(values) + self.last)[: len(values)]
        return held[0] if len(values) == 1 else held

    def mark(self, *values):
        self.last = tuple(values)
        return values[0] if len(values) == 1 else values

    def pin(self, *values):
        held = lax.optimization_barrier(tuple(values) + self.last)[: len(values)]
        return self.mark(*held)


class Ring:
    def __init__(self, line, order, first):
        self.line, self.order, self.taken, self.came = line, order, 0, ()
        self.first = first

    def take(self):
        if self.came:
            self.came = self.order.pin(*self.came)

    def step(self):
        if self.taken < self.line.size - 1:
            self.take()
            self.taken += 1
            self.send(self.taken)
        return self

    def finish(self):
        while self.taken < self.line.size - 1:
            self.step()
        self.take()
        return self.result()


class Gather(Ring):
    def __init__(self, line, order, shard):
        super().__init__(line, order, shard)
        self.low, self.high = [shard], [shard]

    def send(self, step):
        size, axis = self.line.size, self.line.axis
        if self.came:
            self.low[-1], self.high[-1] = self.came
        up = [(k, k + 1) for k in range(step - 1, size - 1)]
        down = [(k + 1, k) for k in range(size - step)]
        self.came = (lax.ppermute(self.low[-1], axis, up), lax.ppermute(self.high[-1], axis, down))
        self.low.append(self.came[0])
        self.high.append(self.came[1])

    def result(self):
        if self.came:
            self.low[-1], self.high[-1] = self.came
        line = self.line
        slots = [self.first]
        for slot in range(1, line.size):
            near = line.me + slot < line.size
            slots.append(jnp.where(near, self.high[slot], self.low[line.size - slot]))
        return slots


class Scatter(Ring):
    def send(self, step):
        size, axis = self.line.size, self.line.axis
        rise, fall = self.first[size - step].astype(F32), self.first[step].astype(F32)
        if self.came:
            rise = rise + self.came[0].astype(F32)
            fall = fall + self.came[1].astype(F32)
        rise, fall = self.order.pin(rise.astype(BF16), fall.astype(BF16))
        low = lax.ppermute(rise, axis, [(k, k + 1) for k in range(step)])
        high = lax.ppermute(fall, axis, [(k, k - 1) for k in range(size - step, size)])
        self.came = (low, high)

    def result(self):
        total = self.first[0].astype(F32)
        for part in self.came:
            total = total + part.astype(F32)
        return total


def rows_of(whole, count):
    rows = whole.shape[0] // count
    return [whole[k * rows : (k + 1) * rows] for k in range(count)]


class Groups:
    def __init__(self, size, order):
        self.size, self.sequence = size, order
        self.chips = size // 2
        self.core = lax.rem(lax.axis_index("dp"), 2)

    def gradient(self, lefts, rights, core, came):
        lefts = list(lefts)
        lefts[0] = self.sequence.after(lefts[0])
        depth = lefts[0].shape[1] // self.size
        blocks = jnp.arange(self.chips, dtype=jnp.int32) * 2 + core
        return self.sequence.mark(weight_grad(lefts, rights, blocks, depth, came))

    def theirs(self, lefts, rights):
        return self.gradient(lefts, rights, 1 - self.core, None)

    def send(self, theirs):
        theirs = self.sequence.after(theirs)
        return lax.ppermute(theirs, "dp", [(k, k ^ 1) for k in range(self.size)])

    def mine(self, lefts, rights, came):
        return self.gradient(lefts, rights, self.core, came)

    def scatter(self, mine):
        mine = self.sequence.after(mine)
        groups = [[2 * chip + core for chip in range(self.chips)] for core in range(2)]
        return lax.psum_scatter(
            mine, "dp", scatter_dimension=0, tiled=True, axis_index_groups=groups
        )


class Total:
    def __init__(self, value, sizes, order):
        self.value, self.order, self.came = value, order, None
        self.rounds = [
            (axis, size, 1 << bit) for axis, size in sizes for bit in range(size.bit_length() - 1)
        ]
        self.step()

    def step(self):
        if self.came is not None:
            self.value = self.order.mark(self.value + self.order.pin(self.came))
            self.came = None
        if self.rounds:
            axis, size, mask = self.rounds.pop(0)
            self.came = lax.ppermute(self.value, axis, [(k, k ^ mask) for k in range(size)])

    def finish(self):
        while self.came is not None:
            self.step()
        return self.value


def shards(
    sizes,
    block_in,
    out_grad,
    segment_ids,
    positions,
    group_token_counts,
    gain_attn,
    w_query,
    w_key,
    w_value,
    w_out,
    gain_mlp,
    w_gate,
    w_up,
    w_down,
):
    order = Order()
    line = Line("tensor", sizes["tensor"])
    groups = Groups(sizes["dp"], order)
    tok_rows, width = block_in.shape
    streams = range(STREAMS)

    qkv_all = lax.all_gather(pack_heads([w_query, w_key, w_value]), "dp", axis=0, tiled=True)
    out_all = lax.all_gather(w_out, "dp", axis=1, tiled=True)
    gate_all = lax.all_gather(w_gate, "dp", axis=0, tiled=True)
    up_all = lax.all_gather(w_up, "dp", axis=0, tiled=True)

    def timed(fn, first, *rest):
        return order.mark(fn(order.after(first), *rest))

    with jax.named_scope("normed_rows"):
        x_float = block_in.astype(F32)
        attn_scale = lax.rsqrt(jnp.mean(x_float * x_float, axis=1, keepdims=True) + EPSILON)
        attn_normed = order.mark((x_float * attn_scale * gain_attn).astype(BF16))
        ring = Gather(line, order, attn_normed).step()
        whole_attn = order.mark(line.in_order(ring.finish()))
    cos, sin = rope_tables(positions)

    with jax.named_scope("live_rows"):
        first_live = lax.axis_index("tensor") * tok_rows
        live = (first_live + jnp.arange(tok_rows) < group_token_counts[0]).astype(BF16)
        live_grad = out_grad * live[:, None]
        live_ring = Gather(line, order, order.after(live_grad)).step()

    with jax.named_scope("attention"):
        qkv = timed(matmul, whole_attn, qkv_all)
        live_ring.step()
        attn, kept, lse = attn_forward(order.after(qkv), cos, sin, segment_ids)
        order.mark(attn)

    attn_slots = line.slots_of(attn)
    attn_of = [
        jnp.concatenate([rows_of(slot, STREAMS)[k] for slot in attn_slots], 0) for k in streams
    ]
    x_of = rows_of(x_float, STREAMS)

    def row_scale(rows):
        return lax.rsqrt(jnp.mean(rows * rows, axis=1, keepdims=True) + EPSILON)

    resid, mlp_scale, whole_mlp = [], [], []

    def mlp_rows(k, total):
        resid.append(x_of[k] + total)
        mlp_scale.append(row_scale(resid[k]))
        return order.mark((resid[k] * mlp_scale[k] * gain_mlp).astype(BF16))

    with jax.named_scope("resid"):
        parts = [timed(matmul, attn_of[k], out_all) for k in streams]
        live_ring.step()
        ring = Scatter(line, order, rows_of(parts[0], line.size)).step()
        ring.step()
        live_slots = live_ring.finish()
        live_of = [
            jnp.concatenate([rows_of(slot, STREAMS)[k] for slot in live_slots], 0) for k in streams
        ]
        ring.step()
        gate_all = order.pin(gate_all)
        down_all = lax.all_gather(order.after(w_down), "dp", axis=1, tiled=True)
        total = ring.finish()

    with jax.named_scope("mlp_rows"):
        ring = Gather(line, order, mlp_rows(0, total)).step()
        ring.step()
        later = Scatter(line, order, rows_of(parts[1], line.size)).step()
        ring.step()
        later.step()
        whole_mlp.append(jnp.concatenate(ring.finish(), 0))
        later.step()

    hidden, acts, d_gate, d_up, d_sums = [], [], [], [], []

    def forward(k):
        made = order.mark(*mlp_forward(order.after(whole_mlp[k]), gate_all, up_all))
        hidden.append(made[0])
        acts.append(made[1:])

    def backward(k):
        made = order.mark(*mlp_backward(order.after(live_of[k]), down_all, *acts[k]))
        d_gate.append(made[0])
        d_up.append(made[1])

    def scatter_input(k):
        part = timed(pair_product, d_gate[k], d_up[k], gate_all, up_all)
        return Scatter(line, order, rows_of(part, line.size)).step()

    d_resid, gains_mlp, whole_resid = [], [], []
    live_parts = rows_of(live_grad, STREAMS)

    def gather_residual(k):
        back, gain_part = norm_back(resid[k], mlp_scale[k], gain_mlp, d_sums[k])
        gains_mlp.append(gain_part)
        d_resid.append(live_parts[k].astype(F32) + back)
        return Gather(line, order, order.mark(d_resid[k].astype(BF16))).step()

    with jax.named_scope("mlp"):
        forward(0)
        ring = Gather(line, order, mlp_rows(1, later.finish())).step()
        whole_mlp.append(jnp.concatenate(ring.finish(), 0))
        backward(0)
        early = scatter_input(0)
        forward(1)
        early.step()
        theirs = groups.theirs(live_of, hidden)
        early.step()
        down_came = groups.send(theirs)
        backward(1)

    with jax.named_scope("grads_mlp"):
        d_sums.append(early.finish())
        ring = gather_residual(0)
        part = timed(pair_product, d_gate[1], d_up[1], gate_all, up_all)
        ring.step()
        later = Scatter(line, order, rows_of(part, line.size)).step()
        down_mine = groups.mine(live_of, hidden, down_came)
        ring.step()
        later.step()
        grad_down = groups.scatter(down_mine)
        theirs = groups.theirs(whole_mlp, d_gate)
        whole_resid.append(jnp.concatenate(ring.finish(), 0))
        later.step()
        gate_came = groups.send(theirs)
        theirs = groups.theirs(whole_mlp, d_up)
        d_sums.append(later.finish())
        ring = gather_residual(1)
        up_came = groups.send(theirs)
        gate_mine = groups.mine(whole_mlp, d_gate, gate_came)
        ring.step()
        grad_down = order.pin(grad_down)
        grad_gate = groups.scatter(gate_mine)
        up_mine = groups.mine(whole_mlp, d_up, up_came)
        ring.step()
        hidden_slots = [rows_of(hidden[k], line.size) for k in streams]
        hidden_rows = jnp.concatenate([part for slot in zip(*hidden_slots) for part in slot], 0)
        down_part = timed(matmul, hidden_rows, down_all)
        d_attn_of = [timed(nt_dot, whole_resid[0], out_all).astype(BF16)]
        whole_resid.append(jnp.concatenate(ring.finish(), 0))
        down_ring = Scatter(line, order, rows_of(down_part, line.size)).step()

    with jax.named_scope("d_attn"):
        d_attn_of.append(timed(nt_dot, whole_resid[1], out_all).astype(BF16))
        d_attn = line.in_order(
            [
                jnp.concatenate(slot, 0)
                for slot in zip(*[rows_of(d_attn_of[k], line.size) for k in streams])
            ]
        )
        order.mark(d_attn)
        grad_gate = order.pin(grad_gate)
        grad_up = groups.scatter(up_mine)
        d_attn = order.after(d_attn)
        d_qkv = order.mark(attn_backward(kept, attn, d_attn, lse, cos, sin, segment_ids))

    with jax.named_scope("grads_attn"):
        qkv_theirs = groups.theirs([whole_attn], [d_qkv])
        down_ring.step()
        qkv_came = groups.send(qkv_theirs)
        out_theirs = groups.theirs(whole_resid, attn_of)
        qkv_mine = groups.mine([whole_attn], [d_qkv], qkv_came)
        down_ring.step()

    with jax.named_scope("d_norm_attn"):
        d_norm_part = timed(nt_dot, d_qkv, qkv_all)
        down_sum = down_ring.finish()
        ring = Scatter(line, order, line.slots_of(d_norm_part)).step()

    with jax.named_scope("grads_attn"):
        grad_up = order.pin(grad_up)
        grad_qkv = groups.scatter(qkv_mine)
        gain_attn_part = order.mark(
            jnp.sum(order.after(d_norm_part) * whole_attn.astype(F32), axis=0) / gain_attn
        )
        everywhere = (("dp", sizes["dp"]), ("tensor", sizes["tensor"]))
        gains = Total(jnp.stack([gain_attn_part, sum(gains_mlp)]), everywhere, order)
        out_came = groups.send(out_theirs)
        grad_down = timed(turned_result, grad_down, w_down.shape[0])
        ring.step()
        gains.step()
        out_mine = groups.mine(whole_resid, attn_of, out_came)
        gains.step()
        grad_gate = timed(turned_result, grad_gate, w_gate.shape[1]).T
        ring.step()
        gains.step()
        grad_up = timed(turned_result, grad_up, w_up.shape[1]).T
        gains.step()
        grad_qkv = order.pin(grad_qkv)
        grad_out = groups.scatter(out_mine)
        grad_query, grad_key, grad_value = order.mark(*unpack_heads(order.after(grad_qkv)))
        d_norm_attn = ring.finish()

    with jax.named_scope("input_grad"):
        d_from_attn, _ = norm_back(x_float, attn_scale, gain_attn, d_norm_attn)
        input_grad = order.mark((jnp.concatenate(d_resid, 0) + d_from_attn).astype(BF16))
    with jax.named_scope("gains"):
        grad_gains = gains.finish()
        grad_gain_attn, grad_gain_mlp = grad_gains[0], grad_gains[1]

    with jax.named_scope("results"):
        block_out = (jnp.concatenate(resid, 0) + down_sum).astype(BF16)
        grad_out = turned_result(grad_out, w_out.shape[0])
    return (
        block_out,
        input_grad,
        grad_gain_attn,
        grad_query,
        grad_key,
        grad_value,
        grad_out,
        grad_gain_mlp,
        grad_gate,
        grad_up,
        grad_down,
    )


def solution(mesh):
    sizes = {axis: mesh.shape[axis] for axis in ("dp", "tensor")}
    rows = P(("dp", "tensor"), None)
    into, outof = P("dp", "tensor"), P("tensor", "dp")
    return jax.shard_map(
        lambda *args: shards(sizes, *args),
        mesh=mesh,
        in_specs=(
            (rows, rows, P("dp"), P("dp"), P("dp"), P())
            + (into, into, into, outof, P(), into, into, outof)
        ),
        out_specs=(rows, rows, P(), into, into, into, outof, P(), into, into, outof),
        check_vma=False,
    )
```

```python
import jax
import jax.numpy as jnp
import numpy as np
from jax import lax
from jax.experimental import pallas as pl
from jax.experimental.pallas import tpu as pltpu
from jax.sharding import PartitionSpec as P

HEAD_DIM = 128
EPSILON = 1e-05
ROPE_BASE = 10000.0
BF16 = jnp.bfloat16
F32 = jnp.float32
ATTN_ROWS = 256
MASKED = -1e30
STREAMS = 2
TILE = 256


def matmul(left, right):
    return jnp.dot(left, right, preferred_element_type=F32)


def allowed_keys(seg_rows, seg_cols, low, high):
    shape = (high - low, high)
    row = lax.broadcasted_iota(jnp.int32, shape, 0) + low
    col = lax.broadcasted_iota(jnp.int32, shape, 1)
    return (seg_rows[low:high, :] == seg_cols[:, :high]) & (col <= row)


def nt_dot(left, right):
    return lax.dot_general(left, right, (((1,), (1,)), ((), ())), preferred_element_type=F32)


def tn_dot(left, right):
    return lax.dot_general(left, right, (((0,), (0,)), ((), ())), preferred_element_type=F32)


def attn_forward_kernel(qkv_ref, cos_ref, sin_ref, segr_ref, segc_ref, out_ref, kept_ref, lse_ref):
    head = pl.program_id(0)
    rows = qkv_ref.shape[0]
    half = HEAD_DIM // 2
    for part in range(2):
        at = slice(part * HEAD_DIM, (part + 1) * HEAD_DIM)
        raw = qkv_ref[:, at]
        turned = raw * cos_ref[...] + pltpu.roll(raw, half, 1) * sin_ref[...]
        kept_ref[:, at] = turned.astype(BF16)
    kept_ref[:, 2 * HEAD_DIM :] = qkv_ref[:, 2 * HEAD_DIM :].astype(BF16)

    @pl.when(head == 0)
    def _():
        lse_ref[...] = jnp.zeros_like(lse_ref)

    block = min(ATTN_ROWS, rows)
    for low in range(0, rows, block):
        high = low + block
        query = kept_ref[low:high, :HEAD_DIM]
        key = kept_ref[:high, HEAD_DIM : 2 * HEAD_DIM]
        value = kept_ref[:high, 2 * HEAD_DIM :]
        scores = nt_dot(query, key) * HEAD_DIM**-0.5
        scores = jnp.where(allowed_keys(segr_ref, segc_ref, low, high), scores, MASKED)
        top = jnp.max(scores, axis=1, keepdims=True)
        weight = jnp.exp(scores - top)
        total = jnp.sum(weight, axis=1, keepdims=True)
        mixed = jnp.dot(weight.astype(BF16), value, preferred_element_type=F32) / total
        out_ref[low:high, :] = mixed.astype(BF16)
        lane = lax.broadcasted_iota(jnp.int32, (block, HEAD_DIM), 1)
        lse_ref[low:high, :] = jnp.where(lane == head, top + jnp.log(total), lse_ref[low:high, :])


def attn_backward_kernel(
    kept_ref, out_ref, dout_ref, lse_ref, cos_ref, sin_ref, segr_ref, segc_ref, grad_ref, dk_ref, dv_ref
):
    head = pl.program_id(0)
    rows = kept_ref.shape[0]
    half = HEAD_DIM // 2
    scale = HEAD_DIM**-0.5
    block = min(ATTN_ROWS, rows)

    def unturn(grad):
        return grad * cos_ref[...] + pltpu.roll(grad * sin_ref[...], half, 1)

    for low in reversed(range(0, rows, block)):
        high = low + block
        query = kept_ref[low:high, :HEAD_DIM]
        key = kept_ref[:high, HEAD_DIM : 2 * HEAD_DIM]
        value = kept_ref[:high, 2 * HEAD_DIM :]
        dout = dout_ref[low:high, :]
        lane = lax.broadcasted_iota(jnp.int32, (block, HEAD_DIM), 1)
        lse = jnp.sum(jnp.where(lane == head, lse_ref[low:high, :], 0.0), axis=1, keepdims=True)
        delta = jnp.sum(dout.astype(F32) * out_ref[low:high, :].astype(F32), axis=1, keepdims=True)
        scores = nt_dot(query, key) * scale - lse
        scores = jnp.where(allowed_keys(segr_ref, segc_ref, low, high), scores, MASKED)
        prob = jnp.exp(scores)
        d_scores = (prob * (nt_dot(dout, value) - delta) * scale).astype(BF16)
        prob = prob.astype(BF16)
        dq = jnp.dot(d_scores, key, preferred_element_type=F32)
        turn = dq * cos_ref[low:high, :] + pltpu.roll(dq * sin_ref[low:high, :], half, 1)
        grad_ref[low:high, :HEAD_DIM] = turn.astype(BF16)
        dk, dv = tn_dot(d_scores, query), tn_dot(prob, dout)
        if high == rows:
            dk_ref[...] = dk
            dv_ref[...] = dv
        else:
            dk_ref[:high, :] += dk
            dv_ref[:high, :] += dv
    grad_ref[:, HEAD_DIM : 2 * HEAD_DIM] = unturn(dk_ref[...]).astype(BF16)
    grad_ref[:, 2 * HEAD_DIM :] = dv_ref[...].astype(BF16)


def attn_specs(rows):
    one = lambda width: pl.BlockSpec((rows, width), lambda h: (0, h))
    fixed = lambda r, c: pl.BlockSpec((r, c), lambda h: (0, 0))
    tables = [fixed(rows, HEAD_DIM), fixed(rows, HEAD_DIM), fixed(rows, 1), fixed(1, rows)]
    return one, fixed, tables


def attn_forward(qkv, cos, sin, seg):
    rows, width = qkv.shape
    heads = width // (3 * HEAD_DIM)
    one, fixed, tables = attn_specs(rows)
    return pl.pallas_call(
        attn_forward_kernel,
        grid=(heads,),
        in_specs=[one(3 * HEAD_DIM)] + tables,
        out_specs=[one(HEAD_DIM), one(3 * HEAD_DIM), fixed(rows, HEAD_DIM)],
        out_shape=[
            jax.ShapeDtypeStruct((rows, heads * HEAD_DIM), BF16),
            jax.ShapeDtypeStruct((rows, width), BF16),
            jax.ShapeDtypeStruct((rows, HEAD_DIM), F32),
        ],
        **big(),
    )(qkv, cos, sin, seg[:, None], seg[None, :])


def attn_backward(kept, out, dout, lse, cos, sin, seg):
    rows, width = kept.shape
    heads = width // (3 * HEAD_DIM)
    one, fixed, tables = attn_specs(rows)
    return pl.pallas_call(
        attn_backward_kernel,
        grid=(heads,),
        in_specs=[one(3 * HEAD_DIM), one(HEAD_DIM), one(HEAD_DIM), fixed(rows, HEAD_DIM)] + tables,
        out_specs=one(3 * HEAD_DIM),
        out_shape=jax.ShapeDtypeStruct((rows, width), BF16),
        scratch_shapes=[pltpu.VMEM((rows, HEAD_DIM), F32)] * 2,
        **big(),
    )(kept, out, dout, lse, cos, sin, seg[:, None], seg[None, :])


def lanes(width):
    return -(-width // 128) * 128


def weight_grad_kernel(pairs, added, order_ref, *refs):
    lefts, rights, out_ref = refs[:pairs], refs[pairs : 2 * pairs], refs[-1]
    width, room = rights[0].shape[1], out_ref.shape[1]
    total = tn_dot(lefts[0][...], rights[0][...])
    for left, right in zip(lefts[1:], rights[1:]):
        total += tn_dot(left[...], right[...])
    if added:
        total += refs[2 * pairs][:, :width].astype(F32)
    out_ref[:, :width] = total.astype(BF16)
    if room > width:
        out_ref[:, width:] = jnp.zeros((out_ref.shape[0], room - width), BF16)


def weight_grad(lefts, rights, order, depth, added=None):
    width = rights[0].shape[1]
    blocks = order.shape[0]
    rows = sum(left.shape[0] for left in lefts)
    specs = [pl.BlockSpec((left.shape[0], depth), lambda i, o: (0, o[i])) for left in lefts]
    specs += [pl.BlockSpec(right.shape, lambda i, o: (0, 0)) for right in rights]
    extra = []
    if added is not None:
        specs.append(pl.BlockSpec((depth, lanes(width)), lambda i, o: (i, 0)))
        extra = [added]
    return pl.pallas_call(
        lambda *refs: weight_grad_kernel(len(lefts), added is not None, *refs),
        grid_spec=pltpu.PrefetchScalarGridSpec(
            num_scalar_prefetch=1,
            grid=(blocks,),
            in_specs=specs,
            out_specs=pl.BlockSpec((depth, lanes(width)), lambda i, o: (i, 0)),
        ),
        out_shape=jax.ShapeDtypeStruct((blocks * depth, lanes(width)), BF16),
        **big(),
    )(order, *lefts, *rights, *extra)


def pack_kernel(*refs):
    *ins, out_ref = refs
    for part, ref in enumerate(ins):
        out_ref[:, part * HEAD_DIM : (part + 1) * HEAD_DIM] = ref[...]


def pack_heads(weights):
    rows, width = weights[0].shape
    count = len(weights)
    return pl.pallas_call(
        pack_kernel,
        grid=(width // HEAD_DIM,),
        in_specs=[pl.BlockSpec((rows, HEAD_DIM), lambda h: (0, h))] * count,
        out_specs=pl.BlockSpec((rows, count * HEAD_DIM), lambda h: (0, h)),
        out_shape=jax.ShapeDtypeStruct((rows, count * width), BF16),
    )(*weights)


def unpack_kernel(ref, *outs):
    for part, out in enumerate(outs):
        out[...] = ref[:, part * HEAD_DIM : (part + 1) * HEAD_DIM].astype(F32)


def unpack_heads(packed):
    rows, width = packed.shape
    span = 3 * HEAD_DIM
    one = pl.BlockSpec((rows, HEAD_DIM), lambda h: (0, h))
    return pl.pallas_call(
        unpack_kernel,
        grid=(width // span,),
        in_specs=[pl.BlockSpec((rows, span), lambda h: (0, h))],
        out_specs=[one] * 3,
        out_shape=[jax.ShapeDtypeStruct((rows, width // 3), F32)] * 3,
    )(packed)


def turned_kernel(in_ref, out_ref):
    out_ref[...] = in_ref[...].astype(F32).T


def turned_result(grad, width):
    rows = grad.shape[0]
    return pl.pallas_call(
        turned_kernel,
        grid=(pl.cdiv(width, TILE),),
        in_specs=[pl.BlockSpec((rows, TILE), lambda i: (0, i))],
        out_specs=pl.BlockSpec((TILE, rows), lambda i: (i, 0)),
        out_shape=jax.ShapeDtypeStruct((width, rows), F32),
    )(grad)


def big():
    return dict(
        compiler_params=pltpu.CompilerParams(
            dimension_semantics=("arbitrary",), vmem_limit_bytes=56 << 20
        ),
        cost_estimate=pl.CostEstimate(flops=1024, bytes_accessed=1024, transcendentals=0),
    )


def mlp_forward_kernel(rows_ref, gate_ref, up_ref, hidden_ref, gate_out, up_out):
    rows = rows_ref[...]
    gate = jnp.dot(rows, gate_ref[...], preferred_element_type=F32)
    up = jnp.dot(rows, up_ref[...], preferred_element_type=F32)
    hidden_ref[...] = (gate * jax.nn.sigmoid(gate) * up).astype(BF16)
    gate_out[...] = gate
    up_out[...] = up


def mlp_forward(rows, gate, up):
    count, depth = rows.shape
    width = gate.shape[1]
    tile = pl.BlockSpec((count, TILE), lambda i: (0, i))
    weight = pl.BlockSpec((depth, TILE), lambda i: (0, i))
    return pl.pallas_call(
        mlp_forward_kernel,
        grid=(pl.cdiv(width, TILE),),
        in_specs=[pl.BlockSpec((count, depth), lambda i: (0, 0)), weight, weight],
        out_specs=[tile] * 3,
        out_shape=[jax.ShapeDtypeStruct((count, width), kind) for kind in (BF16, F32, F32)],
        **big(),
    )(rows, gate, up)


def mlp_backward_kernel(rows_ref, down_ref, gate_ref, up_ref, d_gate_ref, d_up_ref):
    d_hidden = nt_dot(rows_ref[...], down_ref[...])
    gate, up = gate_ref[...], up_ref[...]
    open_gate = jax.nn.sigmoid(gate)
    d_gate_ref[...] = (d_hidden * up * open_gate * (1.0 + gate * (1.0 - open_gate))).astype(BF16)
    d_up_ref[...] = (d_hidden * (gate * open_gate)).astype(BF16)


def mlp_backward(rows, down, gate, up):
    count, depth = rows.shape
    width = down.shape[0]
    tile = pl.BlockSpec((count, TILE), lambda i: (0, i))
    return pl.pallas_call(
        mlp_backward_kernel,
        grid=(pl.cdiv(width, TILE),),
        in_specs=[
            pl.BlockSpec((count, depth), lambda i: (0, 0)),
            pl.BlockSpec((TILE, depth), lambda i: (i, 0)),
            tile,
            tile,
        ],
        out_specs=[tile] * 2,
        out_shape=[jax.ShapeDtypeStruct((count, width), BF16)] * 2,
        **big(),
    )(rows, down, gate, up)


def pair_kernel(first_ref, second_ref, left_ref, right_ref, out_ref):
    total = nt_dot(first_ref[...], left_ref[...]) + nt_dot(second_ref[...], right_ref[...])
    out_ref[...] = total.astype(out_ref.dtype)


def pair_product(first, second, left, right):
    count, depth = first.shape
    width = left.shape[0]
    whole = pl.BlockSpec((count, depth), lambda i: (0, 0))
    weight = pl.BlockSpec((TILE, depth), lambda i: (i, 0))
    return pl.pallas_call(
        pair_kernel,
        grid=(width // TILE,),
        in_specs=[whole, whole, weight, weight],
        out_specs=pl.BlockSpec((count, TILE), lambda i: (0, i)),
        out_shape=jax.ShapeDtypeStruct((count, width), BF16),
        **big(),
    )(first, second, left, right)


def rope_tables(position):
    half_dim = HEAD_DIM // 2
    freq_index = jnp.arange(half_dim).astype(F32)
    frequency = ROPE_BASE ** (-2.0 * freq_index / HEAD_DIM)
    angles = position.astype(F32)[:, None] * frequency[None, :]
    cos, sin = jnp.cos(angles), jnp.sin(angles)
    return jnp.concatenate([cos, cos], 1), jnp.concatenate([-sin, sin], 1)


def norm_back(layer_in, row_inverse_scale, norm_weight, normalized_gradient):
    standardized_gradient = normalized_gradient * norm_weight
    standardized_rows = layer_in * row_inverse_scale
    layer_gradient = row_inverse_scale * (
        standardized_gradient
        - standardized_rows
        * jnp.mean(standardized_gradient * standardized_rows, axis=1, keepdims=True)
    )
    return (layer_gradient, jnp.sum(normalized_gradient * standardized_rows, axis=0))


def after(value, *earlier):
    return lax.optimization_barrier((value,) + earlier)[0]


class Line:
    def __init__(self, axis, size):
        self.axis, self.size = axis, size
        self.me = lax.axis_index(axis)

    def in_order(self, slots):
        rows = slots[0].shape[0]
        whole = jnp.zeros((self.size * rows,) + slots[0].shape[1:], slots[0].dtype)
        for slot, piece in enumerate(slots):
            whole = lax.dynamic_update_slice_in_dim(
                whole, piece, lax.rem(self.me + slot, self.size) * rows, 0
            )
        return whole

    def slots_of(self, whole):
        rows = whole.shape[0] // self.size
        return [
            lax.dynamic_slice_in_dim(whole, lax.rem(self.me + slot, self.size) * rows, rows, 0)
            for slot in range(self.size)
        ]


class Order:
    def __init__(self):
        self.last = ()

    def after(self, *values):
        held = lax.optimization_barrier(tuple(values) + self.last)[: len(values)]
        return held[0] if len(values) == 1 else held

    def mark(self, *values):
        self.last = tuple(values)
        return values[0] if len(values) == 1 else values

    def pin(self, *values):
        held = lax.optimization_barrier(tuple(values) + self.last)[: len(values)]
        return self.mark(*held)


class Ring:
    def __init__(self, line, order, first):
        self.line, self.order, self.taken, self.came = line, order, 0, ()
        self.first = first

    def take(self):
        if self.came:
            self.came = self.order.pin(*self.came)

    def step(self):
        if self.taken < self.line.size - 1:
            self.take()
            self.taken += 1
            self.send(self.taken)
        return self

    def finish(self):
        while self.taken < self.line.size - 1:
            self.step()
        self.take()
        return self.result()


class Gather(Ring):
    def __init__(self, line, order, shard):
        super().__init__(line, order, shard)
        self.low, self.high = [shard], [shard]

    def send(self, step):
        size, axis = self.line.size, self.line.axis
        if self.came:
            self.low[-1], self.high[-1] = self.came
        up = [(k, k + 1) for k in range(step - 1, size - 1)]
        down = [(k + 1, k) for k in range(size - step)]
        self.came = (lax.ppermute(self.low[-1], axis, up), lax.ppermute(self.high[-1], axis, down))
        self.low.append(self.came[0])
        self.high.append(self.came[1])

    def result(self):
        if self.came:
            self.low[-1], self.high[-1] = self.came
        line = self.line
        slots = [self.first]
        for slot in range(1, line.size):
            near = line.me + slot < line.size
            slots.append(jnp.where(near, self.high[slot], self.low[line.size - slot]))
        return slots


class Scatter(Ring):
    def send(self, step):
        size, axis = self.line.size, self.line.axis
        rise, fall = self.first[size - step].astype(F32), self.first[step].astype(F32)
        if self.came:
            rise = rise + self.came[0].astype(F32)
            fall = fall + self.came[1].astype(F32)
        rise, fall = self.order.pin(rise.astype(BF16), fall.astype(BF16))
        low = lax.ppermute(rise, axis, [(k, k + 1) for k in range(step)])
        high = lax.ppermute(fall, axis, [(k, k - 1) for k in range(size - step, size)])
        self.came = (low, high)

    def result(self):
        total = self.first[0].astype(F32)
        for part in self.came:
            total = total + part.astype(F32)
        return total


def rows_of(whole, count):
    rows = whole.shape[0] // count
    return [whole[k * rows : (k + 1) * rows] for k in range(count)]


class Groups:
    def __init__(self, size, order):
        self.size, self.sequence = size, order
        self.chips = size // 2
        self.core = lax.rem(lax.axis_index("dp"), 2)

    def gradient(self, lefts, rights, core, came):
        lefts = list(lefts)
        lefts[0] = self.sequence.after(lefts[0])
        depth = lefts[0].shape[1] // self.size
        blocks = jnp.arange(self.chips, dtype=jnp.int32) * 2 + core
        return self.sequence.mark(weight_grad(lefts, rights, blocks, depth, came))

    def theirs(self, lefts, rights):
        return self.gradient(lefts, rights, 1 - self.core, None)

    def send(self, theirs):
        theirs = self.sequence.after(theirs)
        return lax.ppermute(theirs, "dp", [(k, k ^ 1) for k in range(self.size)])

    def mine(self, lefts, rights, came):
        return self.gradient(lefts, rights, self.core, came)

    def scatter(self, mine):
        mine = self.sequence.after(mine)
        groups = [[2 * chip + core for chip in range(self.chips)] for core in range(2)]
        return lax.psum_scatter(
            mine, "dp", scatter_dimension=0, tiled=True, axis_index_groups=groups
        )


class Total:
    def __init__(self, value, sizes, order):
        self.value, self.order, self.came = value, order, None
        self.rounds = [
            (axis, size, 1 << bit) for axis, size in sizes for bit in range(size.bit_length() - 1)
        ]
        self.step()

    def step(self):
        if self.came is not None:
            self.value = self.order.mark(self.value + self.order.pin(self.came))
            self.came = None
        if self.rounds:
            axis, size, mask = self.rounds.pop(0)
            self.came = lax.ppermute(self.value, axis, [(k, k ^ mask) for k in range(size)])

    def finish(self):
        while self.came is not None:
            self.step()
        return self.value


def shards(
    sizes,
    block_in,
    out_grad,
    segment_ids,
    positions,
    group_token_counts,
    gain_attn,
    w_query,
    w_key,
    w_value,
    w_out,
    gain_mlp,
    w_gate,
    w_up,
    w_down,
):
    order = Order()
    line = Line("tensor", sizes["tensor"])
    groups = Groups(sizes["dp"], order)
    tok_rows, width = block_in.shape
    streams = range(STREAMS)

    qkv_all = lax.all_gather(pack_heads([w_query, w_key, w_value]), "dp", axis=0, tiled=True)
    out_all = lax.all_gather(w_out, "dp", axis=1, tiled=True)
    gate_all = lax.all_gather(w_gate, "dp", axis=0, tiled=True)
    up_all = lax.all_gather(w_up, "dp", axis=0, tiled=True)

    def timed(fn, first, *rest):
        return order.mark(fn(order.after(first), *rest))

    with jax.named_scope("normed_rows"):
        x_float = block_in.astype(F32)
        attn_scale = lax.rsqrt(jnp.mean(x_float * x_float, axis=1, keepdims=True) + EPSILON)
        attn_normed = order.mark((x_float * attn_scale * gain_attn).astype(BF16))
        ring = Gather(line, order, attn_normed).step()
        attn_rows = ring.finish()
    cos, sin = rope_tables(positions)

    with jax.named_scope("live_rows"):
        first_live = lax.axis_index("tensor") * tok_rows
        live = (first_live + jnp.arange(tok_rows) < group_token_counts[0]).astype(BF16)
        live_grad = out_grad * live[:, None]
        live_ring = Gather(line, order, order.after(live_grad)).step()
        whole_attn = order.mark(line.in_order(attn_rows))

    with jax.named_scope("attention"):
        qkv = timed(matmul, whole_attn, qkv_all)
        live_ring.step()
        attn, kept, lse = attn_forward(order.after(qkv), cos, sin, segment_ids)
        order.mark(attn)

    attn_slots = line.slots_of(attn)
    attn_of = [
        jnp.concatenate([rows_of(slot, STREAMS)[k] for slot in attn_slots], 0) for k in streams
    ]
    x_of = rows_of(x_float, STREAMS)

    def row_scale(rows):
        return lax.rsqrt(jnp.mean(rows * rows, axis=1, keepdims=True) + EPSILON)

    resid, mlp_scale, whole_mlp = [], [], []

    def mlp_rows(k, total):
        resid.append(x_of[k] + total)
        mlp_scale.append(row_scale(resid[k]))
        return order.mark((resid[k] * mlp_scale[k] * gain_mlp).astype(BF16))

    with jax.named_scope("resid"):
        parts = [timed(matmul, attn_of[k], out_all) for k in streams]
        live_ring.step()
        ring = Scatter(line, order, rows_of(parts[0], line.size)).step()
        ring.step()
        live_slots = live_ring.finish()
        live_of = [
            jnp.concatenate([rows_of(slot, STREAMS)[k] for slot in live_slots], 0) for k in streams
        ]
        ring.step()
        gate_all = order.pin(gate_all)
        down_all = lax.all_gather(order.after(w_down), "dp", axis=1, tiled=True)
        total = ring.finish()

    with jax.named_scope("mlp_rows"):
        ring = Gather(line, order, mlp_rows(0, total)).step()
        ring.step()
        later = Scatter(line, order, rows_of(parts[1], line.size)).step()
        ring.step()
        later.step()
        whole_mlp.append(jnp.concatenate(ring.finish(), 0))
        later.step()

    hidden, acts, d_gate, d_up, d_sums = [], [], [], [], []

    def forward(k):
        made = order.mark(*mlp_forward(order.after(whole_mlp[k]), gate_all, up_all))
        hidden.append(made[0])
        acts.append(made[1:])

    def backward(k):
        made = order.mark(*mlp_backward(order.after(live_of[k]), down_all, *acts[k]))
        d_gate.append(made[0])
        d_up.append(made[1])

    def scatter_input(k):
        part = timed(pair_product, d_gate[k], d_up[k], gate_all, up_all)
        return Scatter(line, order, rows_of(part, line.size)).step()

    d_resid, gains_mlp, whole_resid = [], [], []
    live_parts = rows_of(live_grad, STREAMS)

    def gather_residual(k):
        back, gain_part = norm_back(resid[k], mlp_scale[k], gain_mlp, d_sums[k])
        gains_mlp.append(gain_part)
        d_resid.append(live_parts[k].astype(F32) + back)
        return Gather(line, order, order.mark(d_resid[k].astype(BF16))).step()

    with jax.named_scope("mlp"):
        forward(0)
        ring = Gather(line, order, mlp_rows(1, later.finish())).step()
        whole_mlp.append(jnp.concatenate(ring.finish(), 0))
        backward(0)
        early = scatter_input(0)
        forward(1)
        early.step()
        theirs = groups.theirs(live_of, hidden)
        early.step()
        down_came = groups.send(theirs)
        backward(1)

    with jax.named_scope("grads_mlp"):
        d_sums.append(early.finish())
        ring = gather_residual(0)
        part = timed(pair_product, d_gate[1], d_up[1], gate_all, up_all)
        ring.step()
        later = Scatter(line, order, rows_of(part, line.size)).step()
        down_mine = groups.mine(live_of, hidden, down_came)
        ring.step()
        later.step()
        grad_down = groups.scatter(down_mine)
        theirs = groups.theirs(whole_mlp, d_gate)
        whole_resid.append(jnp.concatenate(ring.finish(), 0))
        later.step()
        gate_came = groups.send(theirs)
        theirs = groups.theirs(whole_mlp, d_up)
        d_sums.append(later.finish())
        ring = gather_residual(1)
        up_came = groups.send(theirs)
        gate_mine = groups.mine(whole_mlp, d_gate, gate_came)
        ring.step()
        grad_down = order.pin(grad_down)
        grad_gate = groups.scatter(gate_mine)
        up_mine = groups.mine(whole_mlp, d_up, up_came)
        ring.step()
        hidden_slots = [rows_of(hidden[k], line.size) for k in streams]
        hidden_rows = jnp.concatenate([part for slot in zip(*hidden_slots) for part in slot], 0)
        down_part = timed(matmul, hidden_rows, down_all)
        d_attn_of = [timed(nt_dot, whole_resid[0], out_all).astype(BF16)]
        whole_resid.append(jnp.concatenate(ring.finish(), 0))
        down_ring = Scatter(line, order, rows_of(down_part, line.size)).step()

    with jax.named_scope("d_attn"):
        d_attn_of.append(timed(nt_dot, whole_resid[1], out_all).astype(BF16))
        d_attn = line.in_order(
            [
                jnp.concatenate(slot, 0)
                for slot in zip(*[rows_of(d_attn_of[k], line.size) for k in streams])
            ]
        )
        order.mark(d_attn)
        grad_gate = order.pin(grad_gate)
        grad_up = groups.scatter(up_mine)
        d_attn = order.after(d_attn)
        d_qkv = order.mark(attn_backward(kept, attn, d_attn, lse, cos, sin, segment_ids))

    with jax.named_scope("grads_attn"):
        qkv_theirs = groups.theirs([whole_attn], [d_qkv])
        down_ring.step()
        qkv_came = groups.send(qkv_theirs)
        out_theirs = groups.theirs(whole_resid, attn_of)
        qkv_mine = groups.mine([whole_attn], [d_qkv], qkv_came)
        down_ring.step()

    with jax.named_scope("d_norm_attn"):
        d_norm_part = timed(nt_dot, d_qkv, qkv_all)
        down_sum = down_ring.finish()
        ring = Scatter(line, order, line.slots_of(d_norm_part)).step()

    with jax.named_scope("grads_attn"):
        grad_up = order.pin(grad_up)
        grad_qkv = groups.scatter(qkv_mine)
        gain_attn_part = order.mark(
            jnp.sum(order.after(d_norm_part) * whole_attn.astype(F32), axis=0) / gain_attn
        )
        everywhere = (("dp", sizes["dp"]), ("tensor", sizes["tensor"]))
        gains = Total(jnp.stack([gain_attn_part, sum(gains_mlp)]), everywhere, order)
        out_came = groups.send(out_theirs)
        grad_down = timed(turned_result, grad_down, w_down.shape[0])
        ring.step()
        gains.step()
        out_mine = groups.mine(whole_resid, attn_of, out_came)
        gains.step()
        grad_gate = timed(turned_result, grad_gate, w_gate.shape[1]).T
        ring.step()
        gains.step()
        grad_up = timed(turned_result, grad_up, w_up.shape[1]).T
        gains.step()
        grad_qkv = order.pin(grad_qkv)
        grad_out = groups.scatter(out_mine)
        grad_query, grad_key, grad_value = order.mark(*unpack_heads(order.after(grad_qkv)))
        d_norm_attn = ring.finish()

    with jax.named_scope("input_grad"):
        d_from_attn, _ = norm_back(x_float, attn_scale, gain_attn, d_norm_attn)
        input_grad = order.mark((jnp.concatenate(d_resid, 0) + d_from_attn).astype(BF16))
    with jax.named_scope("gains"):
        grad_gains = gains.finish()
        grad_gain_attn, grad_gain_mlp = grad_gains[0], grad_gains[1]

    with jax.named_scope("results"):
        block_out = (jnp.concatenate(resid, 0) + down_sum).astype(BF16)
        grad_out = turned_result(grad_out, w_out.shape[0])
    return (
        block_out,
        input_grad,
        grad_gain_attn,
        grad_query,
        grad_key,
        grad_value,
        grad_out,
        grad_gain_mlp,
        grad_gate,
        grad_up,
        grad_down,
    )


def solution(mesh):
    sizes = {axis: mesh.shape[axis] for axis in ("dp", "tensor")}
    rows = P(("dp", "tensor"), None)
    into, outof = P("dp", "tensor"), P("tensor", "dp")
    return jax.shard_map(
        lambda *args: shards(sizes, *args),
        mesh=mesh,
        in_specs=(
            (rows, rows, P("dp"), P("dp"), P("dp"), P())
            + (into, into, into, outof, P(), into, into, outof)
        ),
        out_specs=(rows, rows, P(), into, into, into, outof, P(), into, into, outof),
        check_vma=False,
    )
```
